32 devices in a mesh: dp: 4 (over z), seq: 8 (over y, x, core).
Axes of the slice: x: 2, y: 2, z: 4, core: 2. Of those that a mesh axis runs over, the one named last changes fastest.
Arguments:
- frames: bfloat16 [4, 1024, 768], P('dp', 'seq'), may hold values from -6 to 6
- segments: int32 [4, 1024], P('dp'), may hold values from 0 to 7, never falling along the last dimension, each value on 1 to 256 neighbouring positions
- conv_weight: float32 [31, 768], replicated, may hold values from -1 to 1
- point_weight: bfloat16 [768, 768], replicated, may hold values from -0.21875 to 0.21875
- router_weight: bfloat16 [768, 8], replicated, may hold values from -0.21875 to 0.21875
- expert_ids: int32 [4, 1024, 2], P('dp', 'seq'), may hold values from 0 to 7, all different within a row; in each aligned block of 128 rows (0 to 127, 128 to 255, ..., all dimensions but the last counted through in order) at most 48 rows name the same one
- expert_in: bfloat16 [8, 768, 3072], P('seq', None, 'dp'), may hold values from -0.21875 to 0.21875
- expert_out: bfloat16 [8, 3072, 768], P('seq', 'dp'), may hold values from -0.109375 to 0.109375
- cotangent: bfloat16 [4, 1024, 768], P('dp', 'seq'), may hold values from -6 to 6
Outputs:
- block_out: bfloat16 [4, 1024, 768], P('dp', 'seq')
- frames_grad: bfloat16 [4, 1024, 768], P('dp', 'seq')
- conv_grad: float32 [31, 768], replicated
- router_grad: float32 [768, 8], replicated
- point_grad: float32 [768, 768], replicated
- expert_in_grad: float32 [8, 768, 3072], P('seq', None, 'dp')
- expert_out_grad: float32 [8, 3072, 768], P('seq', 'dp')
The draws below stay inside these ranges and needn't reach their ends.
Inputs may be any that keep to these rules, and one draw needn't show every extreme that they name: `segments`: within each pack the utterance number never falls; every utterance holds 1 to 256 frames, one exactly 256. `expert_ids`: A frame's two experts differ. Among the frames of one device (aligned blocks of 128 frames of a pack) no expert is named more than 48 times, a bound that some block reaches; every expert is named somewhere.
All inputs are finite; a program needn't handle non-finite values.
Results may differ from the reference program's by a relative error of at most 0.0069.
Values may be sent and summed in bfloat16 or wider, within the bound.
No kernel may reach another device: no remote copies, remote signals or barrier semaphores. Data moves between devices by JAX's collectives and lax.ppermute only.
A program may use at most 128 MiB of HBM per device.

```python
import math
import jax
import jax.numpy as jnp
import numpy as np
from jax import lax

D = 768
FF = 3072
K = 31
SEG_COUNT = 8
TOK_DEV = 128
E = 8
LENGTH = 1024
SEG_MOST = 256
CAP = 48
N_DP = 4
N_SEQ = 8


def steps_of(key, shape, shards, least, high):
    loudness = 1.0
    for dim, blocks in shards:
        heights = jax.random.uniform(jax.random.fold_in(jax.random.fold_in(key, 6), dim), (blocks,), jnp.float32, least / len(shards), high / len(shards))
        loudness = loudness * jnp.repeat(jnp.exp(heights), shape[dim] // blocks).reshape((-1,) + (1,) * (len(shape) - 1 - dim))
    return loudness


def length_profile(number_of, total, most, skew):
    loads = [(1 << 20) // math.isqrt(grade ** skew) + 1 for grade in range(2, number_of + 1)]
    rest, counts = total - most - (number_of - 1), [1] * (number_of - 1)
    while rest > 0:
        free = [i for i in range(number_of - 1) if counts[i] < most]
        pool, left = sum([loads[i] for i in free]), rest
        for i in free:
            extra = min(most - counts[i], max(1, left * loads[i] // pool), rest)
            counts[i] = counts[i] + extra
            rest = rest - extra
    return np.array([most] + counts)


def ragged_sizes(rng, amount, total, most, lean):
    if amount == 2:
        one = jax.random.randint(rng, (), max(1, total - most), min(most, total - 1) + 1)
        return jnp.stack([one, total - one])
    lengths = jnp.asarray(length_profile(amount, total, most, lean), jnp.int32)
    pairs = (amount - 1) // 2
    donor, taker = lengths[1:1 + 2 * pairs:2], lengths[2:2 + 2 * pairs:2]
    margin = jnp.minimum(donor - 1, most - taker)
    passed = jax.random.randint(jax.random.fold_in(rng, 1), (pairs,), 0, 1 << 20) % (margin + 1)
    lengths = lengths.at[1:1 + 2 * pairs:2].set(donor - passed).at[2:2 + 2 * pairs:2].set(taker + passed)
    return lengths[jax.random.permutation(jax.random.fold_in(rng, 2), amount)]


def routed_block(stream_key, own, number, rows, count, top, most, slope):
    ranking = jax.random.permutation(stream_key, count)
    heavy_load, common = portions_of(count, rows * top, most, slope, True), portions_of(count, rows * top, most, slope, False)
    places = jnp.arange(count)

    def named(sizes, turn):
        used = int((sizes > 0).sum())
        fixed = max(1, used // 4)
        moved = fixed + (places - fixed + turn * (used - fixed)) % max(1, count - fixed)
        return jnp.zeros((count,), jnp.int32).at[ranking[jnp.where(places < fixed, places, moved)]].set(jnp.asarray(sizes, jnp.int32))

    sizes = jnp.where(number % 4 == 0, named(heavy_load, number // 4), named(common, number - number // 4 - 1))
    mixed = jax.random.permutation(jax.random.fold_in(own, 3), count)
    donor, taker = mixed[0:count // 2 * 2:2], mixed[1:count // 2 * 2:2]
    slack = jnp.minimum(sizes[donor] - 1, most - sizes[taker]) // 2
    slack = jnp.where((donor == ranking[0]) | (taker == ranking[0]) | (sizes[taker] == 0), 0, jnp.maximum(slack, 0))
    moved = jax.random.randint(jax.random.fold_in(own, 4), (count // 2,), 0, 1 << 20) % (slack + 1)
    sizes = sizes.at[donor].add(-moved).at[taker].add(moved)
    members = jnp.searchsorted(jnp.cumsum(sizes), jnp.arange(rows * top), side="right").astype(jnp.int32)
    grid = members.reshape(top, rows).T
    grid = grid[jax.random.permutation(jax.random.fold_in(own, 1), rows)]
    turn = jax.random.randint(jax.random.fold_in(own, 2), (rows, 1), 0, top)
    return jnp.take_along_axis(grid, (jnp.arange(top)[None, :] + turn) % top, axis=1)


def portions_of(amount, total, limit, skew, full):
    weights = [(1 << 20) // math.isqrt(standing ** skew) + 1 for standing in range(1, amount + 1)]
    largest = limit if full else min(limit, max(-(-total // amount), total * weights[0] // sum(weights)))
    least = 1 if total - largest >= amount - 1 else 0
    counts, spare = [largest] + [least] * (amount - 1), total - largest - least * (amount - 1)
    while spare > 0:
        movable = [i for i in range(1, amount) if counts[i] < largest] or [i for i in range(1, amount) if counts[i] < limit]
        mass, remaining = sum([weights[i] for i in movable]), spare
        for i in movable:
            extra = min(limit - counts[i], max(1, remaining * weights[i] // mass), spare)
            counts[i] = counts[i] + extra
            spare = spare - extra
    return np.array(counts)


def gaussian(stream_key, dims, width, most, cuts=(), kind=jnp.bfloat16):
    gain = steps_of(stream_key, dims, cuts, -0.22, 0.18) if cuts else 1.0
    array = jax.random.normal(stream_key, dims, jnp.float32) * width * gain
    return jnp.minimum(jnp.maximum(array, -most), most).astype(kind)


def setup_inputs(seed: int = 0) -> dict:
    seeds = jax.random.split(jax.random.key(seed), 10)
    frames = gaussian(seeds[0], (N_DP, LENGTH, D), 1.0, 6.0, ((0, 4), (1, 8)))
    segments = jax.vmap(lambda own: jnp.searchsorted(jnp.cumsum(ragged_sizes(own, SEG_COUNT, LENGTH, SEG_MOST, 1)), jnp.arange(LENGTH), side="right"))(jax.random.split(seeds[1], N_DP)).reshape((N_DP, LENGTH)).astype(jnp.int32)
    conv_weight = gaussian(seeds[2], (K, D), K ** -0.5, 1.0, (), jnp.float32)
    point_weight = gaussian(seeds[3], (D, D), D ** -0.5, 0.21875)
    router_weight = gaussian(seeds[4], (D, E), D ** -0.5, 0.21875)
    expert_ids_keys = jax.random.split(jax.random.fold_in(seeds[5], 1), N_DP * LENGTH // TOK_DEV)
    expert_ids_turns = jax.random.permutation(jax.random.fold_in(seeds[5], 3), N_DP * LENGTH // TOK_DEV)
    expert_ids = jax.vmap(lambda own, number: routed_block(jax.random.fold_in(seeds[5], 2), own, number, TOK_DEV, E, 2, CAP, 2))(expert_ids_keys, expert_ids_turns).reshape((N_DP, LENGTH, 2))
    expert_in = gaussian(seeds[6], (E, D, FF), D ** -0.5, 0.21875, ((0, 8), (2, 4)))
    expert_out = gaussian(seeds[7], (E, FF, D), FF ** -0.5, 0.109375, ((0, 8), (1, 4)))
    cotangent = gaussian(seeds[8], (N_DP, LENGTH, D), 1.0, 6.0, ((0, 4), (1, 8)))
    return {"frames": frames, "segments": segments, "conv_weight": conv_weight, "point_weight": point_weight, "router_weight": router_weight, "expert_ids": expert_ids, "expert_in": expert_in, "expert_out": expert_out, "cotangent": cotangent}


def swish_slope(value):
    sigma = jax.nn.sigmoid(value)
    return sigma * (1.0 + value * (1.0 - sigma))


def expert_pass(operands):
    rows_in, grads_in, weight_in, weight_out = operands
    pre_act = jnp.dot(rows_in, weight_in, preferred_element_type=jnp.float32)
    hidden = jax.nn.silu(pre_act).astype(jnp.bfloat16)
    outputs = jnp.dot(hidden, weight_out, preferred_element_type=jnp.float32).astype(jnp.bfloat16)
    grad_hidden = jnp.dot(grads_in, weight_out.T, preferred_element_type=jnp.float32)
    grad_pre = (grad_hidden * swish_slope(pre_act)).astype(jnp.bfloat16)
    grad_wout = jnp.dot(hidden.T, grads_in, preferred_element_type=jnp.float32)
    grad_win = jnp.dot(rows_in.T, grad_pre, preferred_element_type=jnp.float32)
    grad_rows = jnp.dot(grad_pre, weight_in.T, preferred_element_type=jnp.float32).astype(jnp.bfloat16)
    return outputs, grad_rows, grad_win, grad_wout


def reference(frames, segments, conv_weight, point_weight, router_weight, expert_ids, expert_in, expert_out, cotangent):
    reach = (K - 1) // 2
    groups = N_DP
    length = LENGTH
    total_rows = groups * length
    frames_f = frames.astype(jnp.float32)
    padded = jnp.pad(frames_f, ((0, 0), (reach, reach), (0, 0)))
    seg_pad = jnp.pad(segments, ((0, 0), (reach, reach)), constant_values=-1)
    conv_sum = jnp.zeros(frames.shape, jnp.float32)
    for offset in range(K):
        same_seg = (seg_pad[:, offset:offset + length] == segments)[:, :, None]
        conv_sum = conv_sum + conv_weight[offset] * jnp.where(same_seg, padded[:, offset:offset + length], 0.0)
    activated = jax.nn.silu(conv_sum).astype(jnp.bfloat16)
    act_rows = activated.reshape(total_rows, D)
    mixed = (frames_f.reshape(total_rows, D) + jnp.dot(act_rows, point_weight, preferred_element_type=jnp.float32)).astype(jnp.bfloat16)

    choices_all = expert_ids.reshape(total_rows, 2)
    logits_all = jnp.dot(mixed, router_weight, preferred_element_type=jnp.float32)
    pick = (choices_all[:, :, None] == jnp.arange(E, dtype=jnp.int32)).astype(jnp.float32)
    gating = jax.nn.sigmoid(jnp.sum(pick * logits_all[:, None, :], axis=2))

    blocks = choices_all.reshape(groups * N_SEQ, 2 * TOK_DEV)
    one_hot = (blocks[:, :, None] == jnp.arange(E, dtype=jnp.int32)).astype(jnp.int32)
    earlier = (jnp.cumsum(one_hot, axis=1) - one_hot).astype(jnp.int32)
    slot_pos = jnp.sum(earlier * one_hot, axis=2).astype(jnp.int32)
    block_base = (jnp.arange(groups * N_SEQ, dtype=jnp.int32) * CAP)[:, None]
    flat_expert = blocks.reshape(-1)
    flat_row = (block_base + slot_pos).reshape(-1).astype(jnp.int32)

    rows_rep = jnp.repeat(mixed, 2, axis=0)
    buffer = jnp.zeros((E, groups * N_SEQ * CAP, D), jnp.bfloat16).at[flat_expert, flat_row].set(rows_rep)
    cot_rows = cotangent.reshape(total_rows, D).astype(jnp.float32)
    grad_rep = (gating.reshape(-1)[:, None] * jnp.repeat(cot_rows, 2, axis=0)).astype(jnp.bfloat16)
    grad_buffer = jnp.zeros((E, groups * N_SEQ * CAP, D), jnp.bfloat16).at[flat_expert, flat_row].set(grad_rep)

    out_buf, back_buf, grad_win, grad_wout = lax.map(expert_pass, (buffer, grad_buffer, expert_in, expert_out))

    expert_y = out_buf[flat_expert, flat_row].astype(jnp.float32).reshape(total_rows, 2, D)
    expert_back = back_buf[flat_expert, flat_row].astype(jnp.float32).reshape(total_rows, 2, D)
    block_out = (mixed.astype(jnp.float32) + jnp.sum(gating[:, :, None] * expert_y, axis=1)).astype(jnp.bfloat16)

    grad_gate = jnp.sum(cot_rows[:, None, :] * expert_y, axis=2)
    grad_logit = grad_gate * gating * (1.0 - gating)
    logit_cols = jnp.sum(pick * grad_logit[:, :, None], axis=1)
    router_grad = jnp.dot(mixed.astype(jnp.float32).T, logit_cols, precision=lax.Precision.HIGHEST)
    grad_mixed = cot_rows + jnp.sum(expert_back, axis=1) + jnp.dot(logit_cols, router_weight.astype(jnp.float32).T, precision=lax.Precision.HIGHEST)
    grad_mixed_low = grad_mixed.astype(jnp.bfloat16)
    point_grad = jnp.dot(act_rows.T, grad_mixed_low, preferred_element_type=jnp.float32)
    grad_act = jnp.dot(grad_mixed_low, point_weight.T, preferred_element_type=jnp.float32).reshape(groups, length, D)
    grad_conv = (grad_act * swish_slope(conv_sum)).astype(jnp.bfloat16)
    grad_conv_f = grad_conv.astype(jnp.float32)
    grad_pad = jnp.pad(grad_conv_f, ((0, 0), (reach, reach), (0, 0)))
    conv_terms = []
    back_sum = jnp.zeros(frames.shape, jnp.float32)
    for offset in range(K):
        same_seg = (seg_pad[:, offset:offset + length] == segments)[:, :, None]
        conv_terms.append(jnp.sum(grad_conv_f * jnp.where(same_seg, padded[:, offset:offset + length], 0.0), axis=(0, 1)))
        start = 2 * reach - offset
        same_back = (seg_pad[:, start:start + length] == segments)[:, :, None]
        back_sum = back_sum + conv_weight[offset] * jnp.where(same_back, grad_pad[:, start:start + length], 0.0)
    conv_grad = jnp.stack(conv_terms, axis=0)
    frames_grad = (grad_mixed.reshape(groups, length, D) + back_sum).astype(jnp.bfloat16)
    return (block_out.reshape(groups, length, D), frames_grad, conv_grad, router_grad, point_grad, grad_win, grad_wout)
```

```python
import jax
import jax.numpy as jnp
from jax import lax
from jax.experimental import pallas as pl
from jax.experimental.pallas import tpu as pltpu
from jax.sharding import PartitionSpec as P

F32 = jnp.float32
BF16 = jnp.bfloat16
EDGE = 16
LANES = 128


def dot(a, b):
    return jnp.dot(a, b, preferred_element_type=F32)


def sigmoid(value):
    return 1.0 / (1.0 + jnp.exp(-value))


def full(shape):
    zeros = (0,) * len(shape)
    return pl.BlockSpec(shape, lambda *_: zeros)


def fill_padded(scratch, before, own, after):
    rows = own.shape[0]
    scratch[0:EDGE, :] = before[...].astype(F32)
    scratch[EDGE : EDGE + rows, :] = own[...].astype(F32)
    scratch[EDGE + rows : 2 * EDGE + rows, :] = after[...].astype(F32)


def conv_forward_kernel(before, own, after, seg, weight, conv_out, act_out, scratch):
    rows, width = own.shape
    taps = weight.shape[0]
    shift = EDGE - (taps - 1) // 2
    fill_padded(scratch, before, own, after)

    def column(index, carry):
        lanes = pl.ds(pl.multiple_of(index * LANES, LANES), LANES)
        seg_own = seg[EDGE : EDGE + rows, :]
        total = jnp.zeros((rows, LANES), F32)
        for tap in range(taps):
            first = tap + shift
            same = seg[first : first + rows, :] == seg_own
            piece = jnp.where(same, scratch[first : first + rows, lanes], 0.0)
            total = total + weight[tap : tap + 1, lanes] * piece
        conv_out[:, lanes] = total
        act_out[:, lanes] = (total * sigmoid(total)).astype(BF16)
        return carry

    lax.fori_loop(0, width // LANES, column, 0)


def conv_forward(before, own, after, seg, weight):
    rows, width = own.shape
    return pl.pallas_call(
        conv_forward_kernel,
        out_shape=(
            jax.ShapeDtypeStruct((rows, width), F32),
            jax.ShapeDtypeStruct((rows, width), BF16),
        ),
        scratch_shapes=[pltpu.VMEM((rows + 2 * EDGE, width), F32)],
        compiler_params=pltpu.CompilerParams(vmem_limit_bytes=32 << 20),
        name="conv_forward",
    )(before, own, after, seg, weight)


def conv_backward_kernel(before, own, after, seg, weight, grad_mixed, out, scratch):
    rows, width = own.shape
    taps = weight.shape[0]
    shift = EDGE - (taps - 1) // 2
    fill_padded(scratch, before, own, after)

    def column(index, carry):
        lanes = pl.ds(pl.multiple_of(index * LANES, LANES), LANES)
        seg_own = seg[EDGE : EDGE + rows, :]
        total = grad_mixed[:, lanes]
        for tap in range(taps):
            first = tap + shift
            same = seg[first : first + rows, :] == seg_own
            piece = jnp.where(same, scratch[first : first + rows, lanes], 0.0)
            total = total + weight[taps - 1 - tap : taps - tap, lanes] * piece
        out[:, lanes] = total.astype(BF16)
        return carry

    lax.fori_loop(0, width // LANES, column, 0)


def conv_backward(before, own, after, seg, weight, grad_mixed):
    rows, width = own.shape
    return pl.pallas_call(
        conv_backward_kernel,
        out_shape=jax.ShapeDtypeStruct((rows, width), BF16),
        scratch_shapes=[pltpu.VMEM((rows + 2 * EDGE, width), F32)],
        compiler_params=pltpu.CompilerParams(vmem_limit_bytes=32 << 20),
        name="conv_backward",
    )(before, own, after, seg, weight, grad_mixed)


def tail_kernel(*refs):
    count = len(refs) - 11
    parts = refs[:count]
    cot, conv, point_t, before, own, after, seg, grad_mixed, grad_conv, conv_grad, scratch = refs[
        count:
    ]
    rows, width = own.shape
    taps = conv_grad.shape[0] - 1
    shift = EDGE - (taps - 1) // 2
    total = cot[...].astype(F32)
    for part in parts:
        total = total + part[...].astype(F32)
    grad_mixed[...] = total
    grad_act = dot(total.astype(BF16), point_t[...])
    value = conv[...]
    sigma = sigmoid(value)
    grad_conv[...] = (grad_act * (sigma * (1.0 + value * (1.0 - sigma)))).astype(BF16)
    fill_padded(scratch, before, own, after)
    conv_grad[taps : taps + 1, :] = jnp.zeros((1, width), F32)

    def column(index, carry):
        lanes = pl.ds(pl.multiple_of(index * LANES, LANES), LANES)
        seg_own = seg[EDGE : EDGE + rows, :]
        slope = grad_conv[:, lanes].astype(F32)
        for tap in range(taps):
            first = tap + shift
            same = seg[first : first + rows, :] == seg_own
            piece = jnp.where(same, scratch[first : first + rows, lanes], 0.0)
            conv_grad[tap : tap + 1, lanes] = jnp.sum(slope * piece, axis=0, keepdims=True)
        return carry

    lax.fori_loop(0, width // LANES, column, 0)


def tail(parts, cot, conv, point_t, before, own, after, seg, taps):
    rows, width = own.shape
    return pl.pallas_call(
        tail_kernel,
        out_shape=(
            jax.ShapeDtypeStruct((rows, width), F32),
            jax.ShapeDtypeStruct((rows, width), BF16),
            jax.ShapeDtypeStruct((taps + 1, width), F32),
        ),
        scratch_shapes=[pltpu.VMEM((rows + 2 * EDGE, width), F32)],
        compiler_params=pltpu.CompilerParams(vmem_limit_bytes=32 << 20),
        name="tail",
    )(*parts, cot, conv, point_t, before, own, after, seg)


def expert_kernel(
    rows,
    cots,
    weight_in,
    weight_out,
    weight_in_t,
    weight_out_t,
    router_cols,
    router_row,
    gated_out,
    back_out,
    hidden_out,
    grad_pre_out,
    grad_y_out,
    router_out,
):
    row = rows[...]
    width = row.shape[1]
    cot = cots[...].astype(F32)
    gate = sigmoid(dot(row, router_cols[...]))
    gate_wide = jnp.concatenate([gate] * (width // LANES), axis=1)
    grad_y = (gate_wide * cot).astype(BF16)
    grad_y_out[...] = grad_y
    pre = dot(row, weight_in[...])
    sigma = sigmoid(pre)
    hidden = (pre * sigma).astype(BF16)
    hidden_out[...] = hidden
    slope = sigma * (1.0 + pre * (1.0 - sigma))
    grad_pre = (dot(grad_y, weight_out_t[...]) * slope).astype(BF16)
    grad_pre_out[...] = grad_pre
    out = dot(hidden, weight_out[...])
    gated_out[...] = (gate_wide * out).astype(BF16)
    grad_gate = jnp.sum(cot * out, axis=1, keepdims=True)
    grad_logit = grad_gate * (gate * (1.0 - gate))[:, 0:1]
    back = dot(grad_pre, weight_in_t[...]) + grad_logit * router_row[0:1, :]
    back_out[...] = back.astype(BF16)
    partial = jnp.sum(row.astype(F32) * grad_logit, axis=0, keepdims=True)

    @pl.when(pl.program_id(0) == 0)
    def _():
        router_out[...] = jnp.zeros_like(router_out)

    router_out[0:1, :] += partial


def expert(rows, cots, weight_in, weight_out, weight_in_t, weight_out_t, router_cols, router_row):
    total, width = rows.shape
    inner = weight_in.shape[1]
    chunk = 384 if total % 384 == 0 else total

    def tall(columns):
        return pl.BlockSpec((chunk, columns), lambda i: (i, 0))

    return pl.pallas_call(
        expert_kernel,
        grid=(total // chunk,),
        in_specs=[
            tall(width),
            tall(width),
            full(weight_in.shape),
            full(weight_out.shape),
            full(weight_in_t.shape),
            full(weight_out_t.shape),
            full(router_cols.shape),
            full(router_row.shape),
        ],
        out_specs=(
            tall(width),
            tall(width),
            tall(inner),
            tall(inner),
            tall(width),
            full((8, width)),
        ),
        out_shape=(
            jax.ShapeDtypeStruct((total, width), BF16),
            jax.ShapeDtypeStruct((total, width), BF16),
            jax.ShapeDtypeStruct((total, inner), BF16),
            jax.ShapeDtypeStruct((total, inner), BF16),
            jax.ShapeDtypeStruct((total, width), BF16),
            jax.ShapeDtypeStruct((8, width), F32),
        ),
        compiler_params=pltpu.CompilerParams(
            dimension_semantics=("arbitrary",), vmem_limit_bytes=48 << 20
        ),
        name="expert",
    )(rows, cots, weight_in, weight_out, weight_in_t, weight_out_t, router_cols, router_row)


def partners(axis):
    devices = lax.axis_size(axis)
    if devices & (devices - 1):
        raise ValueError("axis size")
    return [[(i, i ^ k) for i in range(devices)] for k in range(1, devices)]


def from_all(array, axis):
    return [array] + [lax.ppermute(array, axis, pairs) for pairs in partners(axis)]


def to_all(arrays, axis):
    return [arrays[0]] + [
        lax.ppermute(part, axis, pairs) for part, pairs in zip(arrays[1:], partners(axis))
    ]


def edges(array, axis):
    devices = lax.axis_size(axis)
    up = [(i, i + 1) for i in range(devices - 1)]
    down = [(j, i) for i, j in up]
    before = lax.ppermute(array[array.shape[0] - EDGE :], axis, up)
    after = lax.ppermute(array[:EDGE], axis, down)
    return before, after


def exchange(array, axis):
    return lax.all_to_all(array, axis, split_axis=0, concat_axis=0, tiled=True)


def sum_parts(parts):
    total = parts[0].astype(F32)
    for part in parts[1:]:
        total = total + part.astype(F32)
    return total


def local(
    frames,
    segments,
    conv_weight,
    point_weight,
    router_weight,
    expert_ids,
    expert_in,
    expert_out,
    cotangent,
):
    rows_here, width = frames.shape[1:]
    taps = conv_weight.shape[0]
    experts = router_weight.shape[1]
    capacity = 3 * rows_here // experts
    packs = lax.axis_size("dp")
    places = lax.axis_size("seq")
    own_frames = frames[0]
    own_cot = cotangent[0]
    before, after = edges(own_frames, "seq")

    seg_line = jnp.pad(segments[0], (EDGE, EDGE), constant_values=-1)
    first_row = lax.axis_index("seq") * rows_here
    seg_here = lax.dynamic_slice_in_dim(seg_line, first_row, rows_here + 2 * EDGE)
    seg = jnp.broadcast_to(seg_here[:, None], (rows_here + 2 * EDGE, LANES))

    ids = jnp.stack(from_all(expert_ids[0].T, "dp"))
    cots = from_all(own_cot, "dp")
    frames_all = from_all(own_frames, "dp")
    span = packs * rows_here
    per_expert = packs * capacity

    named = (ids[:, :, None, :] == jnp.arange(experts, dtype=jnp.int32)[:, None]).astype(BF16)
    earlier = (jnp.arange(rows_here)[:, None] < jnp.arange(rows_here)[None, :]).astype(BF16)
    counts = lax.dot_general(
        named[:, 0] + named[:, 1], earlier, (((2,), (0,)), ((), ())), preferred_element_type=F32
    )
    slot = jnp.sum(named.astype(F32) * counts[:, None], axis=2).astype(jnp.int32)
    pack = jnp.arange(packs, dtype=jnp.int32)[:, None, None]
    position = ids * per_expert + pack * capacity + slot
    rows = jnp.arange(experts * per_expert, dtype=jnp.int32)[:, None]
    table = (
        (rows == position[:, 0].reshape(1, span)) | (rows == position[:, 1].reshape(1, span))
    ).astype(BF16)

    def place(array):
        placed = dot(table, array).astype(BF16)
        return placed.reshape(experts, per_expert, width)

    def collect(buffer):
        return lax.dot_general(
            table,
            buffer.reshape(-1, width),
            (((0,), (0,)), ((), ())),
            preferred_element_type=F32,
        )

    cots_arrived = exchange(place(jnp.concatenate(cots, axis=0)), "seq").reshape(-1, width)

    conv, activated = conv_forward(before, own_frames, after, seg, conv_weight)
    act_all = jnp.concatenate(from_all(activated, "dp"), axis=0)
    mixed_all = (
        jnp.concatenate(frames_all, axis=0).astype(F32) + dot(act_all, point_weight)
    ).astype(BF16)
    rows_arrived = exchange(place(mixed_all), "seq").reshape(-1, width)

    weight_in = expert_in[0]
    weight_out = expert_out[0]
    place_here = lax.axis_index("seq")
    router_col = lax.dynamic_slice_in_dim(router_weight, place_here, 1, axis=1)
    router_cols = jnp.broadcast_to(router_col, (width, LANES))
    router_row = jnp.broadcast_to(router_col.astype(F32).reshape(1, width), (8, width))
    gated, back, hidden, grad_pre, grad_y, router_part = expert(
        rows_arrived,
        cots_arrived,
        weight_in,
        weight_out,
        weight_in.T,
        weight_out.T,
        router_cols,
        router_row,
    )

    back_home = exchange(back.reshape(experts, per_expert, width), "seq")
    gated_home = exchange(gated.reshape(experts, per_expert, width), "seq")
    contract = (((0,), (0,)), ((), ()))
    grad_wout = lax.dot_general(hidden, grad_y, contract, preferred_element_type=F32)[None]
    grad_win = lax.dot_general(rows_arrived, grad_pre, contract, preferred_element_type=F32)[None]

    back_part = collect(back_home)
    back_low = back_part.astype(BF16).reshape(packs, rows_here, width)
    back_parts = to_all([back_low[k] for k in range(packs)], "dp")
    with_cot = jnp.concatenate(
        [(back_part[:rows_here] + own_cot.astype(F32)).astype(BF16)]
        + [back_low[k] for k in range(1, packs)],
        axis=0,
    )
    point_part = lax.dot_general(act_all, with_cot, contract, preferred_element_type=F32)

    spot = (jnp.arange(experts, dtype=jnp.int32) == place_here)[:, None]
    router_rows = jnp.where(spot, router_part[0:1, :], 0.0)
    used = width + experts
    step = EDGE * places
    padding = -used % step
    shared = jnp.concatenate(
        [point_part.astype(BF16), router_rows.astype(BF16), jnp.zeros((padding, width), BF16)],
        axis=0,
    ).reshape(places, (used + padding) // places, width)
    share = jnp.sum(exchange(shared, "seq").astype(F32), axis=0)
    share = sum_parts(from_all(share.astype(BF16), "dp")).astype(BF16)
    spread = exchange(jnp.broadcast_to(share[None], (places,) + share.shape), "seq")
    spread = spread.reshape(-1, width).astype(F32)
    point_grad = spread[:width]
    router_grad = spread[width:used].T

    grad_mixed, grad_conv, conv_part = tail(
        back_parts, own_cot, conv, point_weight.T, before, own_frames, after, seg, taps
    )
    grad_before, grad_after = edges(grad_conv, "seq")
    frames_grad = conv_backward(grad_before, grad_conv, grad_after, seg, conv_weight, grad_mixed)

    conv_seq = exchange(
        jnp.broadcast_to(conv_part.astype(BF16)[None], (places,) + conv_part.shape), "seq"
    )
    conv_sum = jnp.sum(conv_seq.astype(F32), axis=0).astype(BF16)
    conv_grad = sum_parts(from_all(conv_sum, "dp"))[:taps]

    gated_part = collect(gated_home).astype(BF16).reshape(packs, rows_here, width)
    gated_parts = to_all([gated_part[k] for k in range(packs)], "dp")
    block_out = (mixed_all[:rows_here].astype(F32) + sum_parts(gated_parts)).astype(BF16)
    return (
        block_out[None],
        frames_grad[None],
        conv_grad,
        router_grad,
        point_grad,
        grad_win,
        grad_wout,
    )


def solution(mesh):
    placed = (
        P("dp", "seq", None),
        P("dp", None),
        P(),
        P(),
        P(),
        P("dp", "seq", None),
        P("seq", None, "dp"),
        P("seq", "dp", None),
        P("dp", "seq", None),
    )
    return jax.shard_map(
        local,
        mesh=mesh,
        in_specs=placed,
        out_specs=(
            P("dp", "seq", None),
            P("dp", "seq", None),
            P(),
            P(),
            P(),
            P("seq", None, "dp"),
            P("seq", "dp", None),
        ),
        check_vma=False,
    )
```

```python
import jax
import jax.numpy as jnp
from jax import lax
from jax.experimental import pallas as pl
from jax.experimental.pallas import tpu as pltpu
from jax.sharding import PartitionSpec as P

F32 = jnp.float32
BF16 = jnp.bfloat16
EDGE = 16
LANES = 128
SUB = 384
PARAMS = pltpu.CompilerParams(vmem_limit_bytes=56 << 20)


def shape(dims, dtype):
    return jax.ShapeDtypeStruct(dims, dtype)


def dot(a, b):
    return jnp.dot(a, b, preferred_element_type=F32)


def dot_rows(a, b):
    return lax.dot_general(a, b, (((0,), (0,)), ((), ())), preferred_element_type=F32)


def sigmoid(value):
    return 1.0 / (1.0 + jnp.exp(-value))


def fill_padded(scratch, before, own, after):
    rows = own.shape[0]
    scratch[0:EDGE, :] = before[...].astype(F32)
    scratch[EDGE : EDGE + rows, :] = own[...].astype(F32)
    scratch[EDGE + rows : 2 * EDGE + rows, :] = after[...].astype(F32)


def conv_forward_kernel(
    before, own, after, seg, weight, point, ids, conv_out, act_out, packet, scratch
):
    rows, width = own.shape
    taps = weight.shape[0]
    shift = EDGE - (taps - 1) // 2
    fill_padded(scratch, before, own, after)

    def column(index, carry):
        lanes = pl.ds(pl.multiple_of(index * LANES, LANES), LANES)
        seg_own = seg[EDGE : EDGE + rows, :]
        total = jnp.zeros((rows, LANES), F32)
        for tap in range(taps):
            first = tap + shift
            same = seg[first : first + rows, :] == seg_own
            piece = jnp.where(same, scratch[first : first + rows, lanes], 0.0)
            total = total + weight[tap : tap + 1, lanes] * piece
        conv_out[:, lanes] = total
        act_out[:, lanes] = (total * sigmoid(total)).astype(BF16)
        return carry

    lax.fori_loop(0, width // LANES, column, 0)
    packet[:rows, :] = (own[...].astype(F32) + dot(act_out[...], point[...])).astype(BF16)
    packet[rows:, :] = ids[...]


def conv_forward(before, own, after, seg, weight, point, ids):
    rows, width = own.shape
    return pl.pallas_call(
        conv_forward_kernel,
        out_shape=(
            shape((rows, width), F32),
            shape((rows, width), BF16),
            shape((rows + EDGE, width), BF16),
        ),
        scratch_shapes=[pltpu.VMEM((rows + 2 * EDGE, width), F32)],
        compiler_params=PARAMS,
        name="conv_forward",
    )(before, own, after, seg, weight, point, ids)


def conv_backward_kernel(before, own, after, seg, weight, grad_mixed, out, scratch):
    rows, width = own.shape
    taps = weight.shape[0]
    shift = EDGE - (taps - 1) // 2
    fill_padded(scratch, before, own, after)

    def column(index, carry):
        lanes = pl.ds(pl.multiple_of(index * LANES, LANES), LANES)
        seg_own = seg[EDGE : EDGE + rows, :]
        total = grad_mixed[:, lanes]
        for tap in range(taps):
            first = tap + shift
            same = seg[first : first + rows, :] == seg_own
            piece = jnp.where(same, scratch[first : first + rows, lanes], 0.0)
            total = total + weight[taps - 1 - tap : taps - tap, lanes] * piece
        out[:, lanes] = total.astype(BF16)
        return carry

    lax.fori_loop(0, width // LANES, column, 0)


def conv_backward(before, own, after, seg, weight, grad_mixed):
    rows, width = own.shape
    return pl.pallas_call(
        conv_backward_kernel,
        out_shape=shape((rows, width), BF16),
        scratch_shapes=[pltpu.VMEM((rows + 2 * EDGE, width), F32)],
        compiler_params=PARAMS,
        name="conv_backward",
    )(before, own, after, seg, weight, grad_mixed)


def tail(
    parts, cot, conv, act, point_t, before, own, after, seg, spot, router_part, core, places, taps
):
    rows, width = own.shape
    experts = spot.shape[0]
    shift = EDGE - (taps - 1) // 2
    groups = places // 2
    used = width // places
    lead = -(-used // EDGE) * EDGE
    extra = -(-(taps + 1 + experts) // EDGE)
    count = len(parts)
    pieces = (groups, lead + EDGE, width)

    def kernel(core, *refs):
        parts = refs[:count]
        cot, conv, act, point_t, before, own, after, seg, spot, router_part = refs[
            count : count + 10
        ]
        grad_mixed, grad_conv, mine, theirs, scratch, shared = refs[count + 10 :]
        total = cot[...].astype(F32)
        for part in parts:
            total = total + part[...].astype(F32)
        grad_mixed[...] = total
        low = total.astype(BF16)
        grad_act = dot(low, point_t[...])
        value = conv[...]
        sigma = sigmoid(value)
        grad_conv[...] = (grad_act * (sigma * (1.0 + value * (1.0 - sigma)))).astype(BF16)
        fill_padded(scratch, before, own, after)
        point = dot_rows(act[...], low).astype(BF16)
        for index in range(places):
            side, group = divmod(index, groups)
            shared[side, group] = jnp.zeros(pieces[1:], BF16)
            shared[side, group, 0:used, :] = point[index * used : (index + 1) * used]

        def column(index, carry):
            lanes = pl.ds(pl.multiple_of(index * LANES, LANES), LANES)
            seg_own = seg[EDGE : EDGE + rows, :]
            slope = grad_conv[:, lanes].astype(F32)
            sums = []
            for tap in range(taps):
                first = tap + shift
                same = seg[first : first + rows, :] == seg_own
                piece = jnp.where(same, scratch[first : first + rows, lanes], 0.0)
                sums.append(jnp.sum(slope * piece, axis=0, keepdims=True))
            sums.append(jnp.zeros((1, LANES), F32))
            sums.append(spot[...] * router_part[0:1, lanes])
            missing = extra * EDGE - (taps + 1 + experts)
            if missing:
                sums.append(jnp.zeros((missing, LANES), F32))
            small = jnp.concatenate(sums, axis=0).astype(BF16)
            for index in range(extra):
                side, group = divmod(index, groups)
                shared[side, group, lead : lead + EDGE, lanes] = small[
                    index * EDGE : (index + 1) * EDGE
                ]
            return carry

        lax.fori_loop(0, width // LANES, column, 0)
        mine[...] = shared[core[0]]
        theirs[...] = shared[1 - core[0]]

    return pl.pallas_call(
        kernel,
        in_specs=[pl.BlockSpec(memory_space=pltpu.SMEM)]
        + [pl.BlockSpec(memory_space=pltpu.VMEM)] * (count + 10),
        out_shape=(
            shape((rows, width), F32),
            shape((rows, width), BF16),
            shape(pieces, BF16),
            shape(pieces, BF16),
        ),
        scratch_shapes=[
            pltpu.VMEM((rows + 2 * EDGE, width), F32),
            pltpu.VMEM((2,) + pieces, BF16),
        ],
        compiler_params=PARAMS,
        name="tail",
    )(core, *parts, cot, conv, act, point_t, before, own, after, seg, spot, router_part)


def table_of(ids, experts, capacity):
    rows = ids.shape[1]
    ids = ids[0:2, :].astype(F32)
    expert = lax.broadcasted_iota(jnp.int32, (experts, rows), 0).astype(F32)
    named = [jnp.where(expert == ids[j : j + 1, :], 1.0, 0.0) for j in range(2)]
    earlier = lax.broadcasted_iota(jnp.int32, (rows, rows), 0)
    earlier = earlier < lax.broadcasted_iota(jnp.int32, (rows, rows), 1)
    counts = dot((named[0] + named[1]).astype(BF16), jnp.where(earlier, 1.0, 0.0).astype(BF16))
    row = lax.broadcasted_iota(jnp.int32, (experts * capacity, rows), 0).astype(F32)
    table = jnp.zeros((experts * capacity, rows), F32)
    for j in range(2):
        slot = jnp.sum(named[j] * counts, axis=0, keepdims=True)
        table = jnp.where(row == ids[j : j + 1, :] * capacity + slot, 1.0, table)
    return table.astype(BF16)


def place_all(packets, experts, capacity, pack_here):
    count = len(packets)
    rows, width = packets[0].shape[0] - EDGE, packets[0].shape[1]
    per_expert = count * capacity

    def kernel(pack_here, *refs):
        packets, out, tables = refs[:count], refs[count], refs[count + 1]
        for k, packet in enumerate(packets):
            table = table_of(packet[rows:, :rows], experts, capacity)
            tables[k] = table
            placed = dot(table, packet[:rows, :]).astype(BF16)
            first = (pack_here[0] ^ k) * capacity
            for expert in range(experts):
                start = pl.multiple_of(expert * per_expert + first, EDGE)
                piece = placed[expert * capacity : (expert + 1) * capacity]
                out[pl.ds(start, capacity), :] = piece

    return pl.pallas_call(
        kernel,
        in_specs=[pl.BlockSpec(memory_space=pltpu.SMEM)]
        + [pl.BlockSpec(memory_space=pltpu.VMEM)] * count,
        out_shape=(
            shape((experts * per_expert, width), BF16),
            shape((count, experts * capacity, rows), BF16),
        ),
        compiler_params=PARAMS,
        name="place_all",
    )(pack_here, *packets)


def place_more(tables, arrays, experts, capacity, pack_here):
    count, _, rows = tables.shape
    width = arrays[0].shape[1]
    per_expert = count * capacity

    def kernel(pack_here, tables, *refs):
        out = refs[count]
        for k, array in enumerate(refs[:count]):
            placed = dot(tables[k], array[...]).astype(BF16)
            first = (pack_here[0] ^ k) * capacity
            for expert in range(experts):
                start = pl.multiple_of(expert * per_expert + first, EDGE)
                piece = placed[expert * capacity : (expert + 1) * capacity]
                out[pl.ds(start, capacity), :] = piece

    return pl.pallas_call(
        kernel,
        in_specs=[pl.BlockSpec(memory_space=pltpu.SMEM)]
        + [pl.BlockSpec(memory_space=pltpu.VMEM)] * (count + 1),
        out_shape=shape((experts * per_expert, width), BF16),
        compiler_params=PARAMS,
        name="place_more",
    )(pack_here, tables, *arrays)


def finish(tables, buffer, packet):
    rows = tables.shape[2]
    width = buffer.shape[1]

    def kernel(tables, buffer, packet, out):
        summed = dot_rows(tables[0], buffer[...])
        out[...] = (packet[:rows, :].astype(F32) + summed).astype(BF16)

    return pl.pallas_call(
        kernel,
        out_shape=shape((rows, width), BF16),
        compiler_params=PARAMS,
        name="finish",
    )(tables, buffer, packet)


def collect(tables, buffer, experts, capacity, pack_here):
    count, _, rows = tables.shape
    width = buffer.shape[1]
    per_expert = count * capacity

    def kernel(pack_here, tables, buffer, *outs):
        for k, out in enumerate(outs):
            first = (pack_here[0] ^ k) * capacity
            starts = [
                pl.multiple_of(expert * per_expert + first, EDGE) for expert in range(experts)
            ]
            pieces = [buffer[pl.ds(start, capacity), :] for start in starts]
            out[...] = dot_rows(tables[k], jnp.concatenate(pieces, axis=0)).astype(BF16)

    return pl.pallas_call(
        kernel,
        in_specs=[pl.BlockSpec(memory_space=pltpu.SMEM)]
        + [pl.BlockSpec(memory_space=pltpu.VMEM)] * 2,
        out_shape=[shape((rows, width), BF16)] * count,
        compiler_params=PARAMS,
        name="collect",
    )(pack_here, tables, buffer)


def expert_specs(rows, inner):
    places, packs, capacity, width = rows.shape
    group = max(1, SUB // (packs * capacity))
    chunk = group * packs * capacity
    by_place = pl.BlockSpec((group, packs, capacity, width), lambda i: (i, 0, 0, 0))
    by_pack = pl.BlockSpec((packs, group, capacity, width), lambda i: (0, i, 0, 0))

    def flat(columns):
        return pl.BlockSpec((chunk, columns), lambda i: (i, 0))

    def full(dims):
        return pl.BlockSpec(dims, lambda i: (0,) * len(dims))

    return group, chunk, by_place, by_pack, flat, full


def expert_forward(rows, weight_in, weight_out, router_cols):
    places, packs, capacity, width = rows.shape
    inner = weight_in.shape[1]
    total = places * packs * capacity
    group, chunk, by_place, by_pack, flat, full = expert_specs(rows, inner)
    cells = [(place, pack) for place in range(group) for pack in range(packs)]

    def kernel(rows, w_in, w_out, r_cols, gated_out, hidden_out, slope_out, gate_out):
        row = rows[...].reshape(chunk, width)
        gate = sigmoid(dot(row, r_cols[...]))
        gate_out[...] = gate
        pre = dot(row, w_in[...])
        sigma = sigmoid(pre)
        hidden = (pre * sigma).astype(BF16)
        hidden_out[...] = hidden
        slope_out[...] = (sigma * (1.0 + pre * (1.0 - sigma))).astype(BF16)
        gate_wide = jnp.concatenate([gate] * (width // LANES), axis=1)
        gated = (gate_wide * dot(hidden, w_out[...])).astype(BF16)
        for index, (place, pack) in enumerate(cells):
            gated_out[pack, place] = gated[index * capacity : (index + 1) * capacity]

    return pl.pallas_call(
        kernel,
        grid=(places // group,),
        in_specs=[by_place, full(weight_in.shape), full(weight_out.shape)]
        + [full(router_cols.shape)],
        out_specs=(by_pack, flat(inner), flat(inner), flat(LANES)),
        out_shape=(
            shape((packs, places, capacity, width), BF16),
            shape((total, inner), BF16),
            shape((total, inner), BF16),
            shape((total, LANES), F32),
        ),
        compiler_params=PARAMS,
        name="expert_forward",
    )(rows, weight_in, weight_out, router_cols)


def expert_backward(rows, cots, gated, slope, gate, weight_in_t, weight_out_t, router_row):
    places, packs, capacity, width = rows.shape
    inner = weight_in_t.shape[0]
    total = places * packs * capacity
    group, chunk, by_place, by_pack, flat, full = expert_specs(rows, inner)
    cells = [(place, pack) for place in range(group) for pack in range(packs)]

    def kernel(
        rows,
        cots,
        gated,
        slope,
        gate,
        w_in_t,
        w_out_t,
        r_row,
        back_out,
        grad_pre_out,
        grad_y_out,
        router_out,
    ):
        row = rows[...].reshape(chunk, width)
        cot = cots[...].reshape(chunk, width).astype(F32)
        gates = gate[...]
        gate_wide = jnp.concatenate([gates] * (width // LANES), axis=1)
        grad_y = (gate_wide * cot).astype(BF16)
        grad_y_out[...] = grad_y
        grad_pre = (dot(grad_y, w_out_t[...]) * slope[...].astype(F32)).astype(BF16)
        grad_pre_out[...] = grad_pre
        out = jnp.concatenate([gated[pack, place] for place, pack in cells], axis=0)
        grad_gate = jnp.sum(cot * out.astype(F32), axis=1, keepdims=True)
        grad_logit = grad_gate * (1.0 - gates)[:, 0:1]
        back = dot(grad_pre, w_in_t[...]) + grad_logit * r_row[0:1, :]
        back_out[...] = back.astype(BF16).reshape(rows.shape)
        partial = jnp.sum(row.astype(F32) * grad_logit, axis=0, keepdims=True)

        @pl.when(pl.program_id(0) == 0)
        def _():
            router_out[...] = jnp.zeros_like(router_out)

        router_out[0:1, :] += partial

    return pl.pallas_call(
        kernel,
        grid=(places // group,),
        in_specs=[by_place, by_place, by_pack, flat(inner), flat(LANES)]
        + [full(weight_in_t.shape), full(weight_out_t.shape), full(router_row.shape)],
        out_specs=(by_place, flat(inner), flat(width), full((8, width))),
        out_shape=(
            shape(rows.shape, BF16),
            shape((total, inner), BF16),
            shape((total, width), BF16),
            shape((8, width), F32),
        ),
        compiler_params=PARAMS,
        name="expert_backward",
    )(rows, cots, gated, slope, gate, weight_in_t, weight_out_t, router_row)


def add_pieces(mine, theirs, group):
    groups, size, width = mine.shape

    def kernel(group, mine, theirs, *outs):
        for index, out in enumerate(outs):
            here = group[0] ^ index
            out[...] = (mine[here].astype(F32) + theirs[here].astype(F32)).astype(BF16)

    return pl.pallas_call(
        kernel,
        in_specs=[pl.BlockSpec(memory_space=pltpu.SMEM)]
        + [pl.BlockSpec(memory_space=pltpu.VMEM)] * 2,
        out_shape=[shape((size, width), BF16)] * groups,
        compiler_params=PARAMS,
        name="add_pieces",
    )(group, mine, theirs)


def spread(own, other, group, core, used):
    count = len(own)
    size, width = own[0].shape

    def kernel(where, *refs):
        point, small = refs[2 * count :]
        for index in range(2 * count):
            side = where[1] if index < count else 1 - where[1]
            place = side * count + (where[0] ^ (index % count))
            piece = refs[index][...].astype(F32)
            point[place] = piece[:used]
            small[place] = piece[size - EDGE :]

    return pl.pallas_call(
        kernel,
        in_specs=[pl.BlockSpec(memory_space=pltpu.SMEM)]
        + [pl.BlockSpec(memory_space=pltpu.VMEM)] * (2 * count),
        out_shape=(
            shape((2 * count, used, width), F32),
            shape((2 * count, EDGE, width), F32),
        ),
        compiler_params=PARAMS,
        name="spread",
    )(jnp.stack([group, core]), *own, *other)


def swap(array, axis, k):
    devices = lax.axis_size(axis)
    return lax.ppermute(array, axis, [(i, i ^ k) for i in range(devices)])


def from_all(array, axis):
    return [array] + [swap(array, axis, k) for k in range(1, lax.axis_size(axis))]


def to_all(arrays, axis):
    return [part if k == 0 else swap(part, axis, k) for k, part in enumerate(arrays)]


def exchange(array, axis):
    return lax.all_to_all(array, axis, split_axis=0, concat_axis=0, tiled=True)


def after_all(array, others):
    return lax.optimization_barrier((array, tuple(others)))[0]


def edges(array, axis):
    devices = lax.axis_size(axis)
    up = [(i, i + 1) for i in range(devices - 1)]
    down = [(j, i) for i, j in up]
    before = lax.ppermute(array[array.shape[0] - EDGE :], axis, up)
    after = lax.ppermute(array[:EDGE], axis, down)
    return before, after


def sum_parts(parts):
    total = parts[0].astype(F32)
    for part in parts[1:]:
        total = total + part.astype(F32)
    return total


def local(
    frames,
    segments,
    conv_weight,
    point_weight,
    router_weight,
    expert_ids,
    expert_in,
    expert_out,
    cotangent,
):
    rows_here, width = frames.shape[1:]
    taps = conv_weight.shape[0]
    experts = router_weight.shape[1]
    capacity = -(-3 * rows_here // experts // EDGE) * EDGE
    packs = lax.axis_size("dp")
    places = lax.axis_size("seq")
    place_here = lax.axis_index("seq")
    pack_here = lax.axis_index("dp")[None]
    own_frames = frames[0]
    own_cot = cotangent[0]
    before, after = edges(own_frames, "seq")

    seg_line = jnp.pad(segments[0], (EDGE, EDGE), constant_values=-1)
    seg_here = lax.dynamic_slice_in_dim(seg_line, place_here * rows_here, rows_here + 2 * EDGE)
    seg = jnp.broadcast_to(seg_here[:, None], (rows_here + 2 * EDGE, LANES))

    ids = jnp.pad(expert_ids[0].T.astype(BF16), ((0, EDGE - 2), (0, width - rows_here)))
    conv, activated, packet = conv_forward(
        before, own_frames, after, seg, conv_weight, point_weight, ids
    )
    packets = from_all(packet, "dp")
    placed, tables = place_all(packets, experts, capacity, pack_here)
    rows = exchange(placed.reshape(places, packs * capacity, width), "seq")
    cots = from_all(after_all(own_cot, packets), "dp")
    cots_placed = place_more(tables, cots, experts, capacity, pack_here)
    cots_placed, rows = lax.optimization_barrier((cots_placed, rows))
    cot_rows = exchange(cots_placed.reshape(places, packs * capacity, width), "seq")

    weight_in = expert_in[0]
    weight_out = expert_out[0]
    router_col = lax.dynamic_slice_in_dim(router_weight, place_here, 1, axis=1)
    router_cols = jnp.broadcast_to(router_col, (width, LANES))
    router_row = jnp.broadcast_to(router_col.astype(F32).reshape(1, width), (8, width))
    rows = rows.reshape(places, packs, capacity, width)
    gated, hidden, slope, gate = expert_forward(rows, weight_in, weight_out, router_cols)
    gated_sum = lax.psum_scatter(
        gated.reshape(packs * places, capacity, width), "dp", scatter_dimension=0, tiled=True
    )
    back, grad_pre, grad_y, router_part = expert_backward(
        rows,
        cot_rows.reshape(rows.shape),
        gated,
        slope,
        gate,
        weight_in.T,
        weight_out.T,
        router_row,
    )
    back_home = exchange(back.reshape(places, packs * capacity, width), "seq")
    grad_wout = dot_rows(hidden, grad_y)
    grad_win = dot_rows(rows.reshape(-1, width), grad_pre)
    back_home, (grad_wout, grad_win) = lax.optimization_barrier(
        (back_home, (grad_wout, grad_win))
    )
    back_parts = collect(tables, back_home.reshape(-1, width), experts, capacity, pack_here)
    back_own = to_all(back_parts, "dp")
    gated_home = exchange(after_all(gated_sum, (back_home,)), "seq").reshape(-1, width)
    block_out = finish(tables, gated_home, packet)

    core = place_here % 2
    group = place_here // 2
    groups = places // 2
    spot = jnp.broadcast_to(
        (jnp.arange(experts, dtype=jnp.int32) == place_here).astype(F32)[:, None],
        (experts, LANES),
    )
    grad_mixed, grad_conv, mine, theirs = tail(
        back_own,
        own_cot,
        conv,
        activated,
        point_weight.T,
        before,
        own_frames,
        after,
        seg,
        spot,
        router_part,
        core[None],
        places,
        taps,
    )
    pieces = add_pieces(mine, swap(theirs, "seq", 1), group[None])
    pieces = [pieces[0]] + [swap(pieces[m], "seq", 2 * m) for m in range(1, groups)]
    share = sum_parts(pieces).astype(BF16)
    grad_before, grad_after = edges(grad_conv, "seq")
    frames_grad = conv_backward(grad_before, grad_conv, grad_after, seg, conv_weight, grad_mixed)
    share, frames_grad, block_out = lax.optimization_barrier((share, frames_grad, block_out))
    share = sum_parts(from_all(share, "dp")).astype(BF16)
    own_half = [share] + [swap(share, "seq", 2 * m) for m in range(1, groups)]
    other_half = [swap(part, "seq", 1) for part in own_half]
    point_grad, small = spread(own_half, other_half, group, core, width // places)
    point_grad = point_grad.reshape(width, width)
    small = small.reshape(-1, width)
    conv_grad = small[:taps]
    router_grad = small[taps + 1 : taps + 1 + experts].T

    return (
        block_out[None],
        frames_grad[None],
        conv_grad,
        router_grad,
        point_grad,
        grad_win[None],
        grad_wout[None],
    )


def solution(mesh):
    placed = (
        P("dp", "seq", None),
        P("dp", None),
        P(),
        P(),
        P(),
        P("dp", "seq", None),
        P("seq", None, "dp"),
        P("seq", "dp", None),
        P("dp", "seq", None),
    )
    return jax.shard_map(
        local,
        mesh=mesh,
        in_specs=placed,
        out_specs=(
            P("dp", "seq", None),
            P("dp", "seq", None),
            P(),
            P(),
            P(),
            P("seq", None, "dp"),
            P("seq", "dp", None),
        ),
        check_vma=False,
    )
```

```python
import jax
import jax.numpy as jnp
from jax import lax
from jax.experimental import pallas as pl
from jax.experimental.pallas import tpu as pltpu
from jax.sharding import PartitionSpec as P

F32 = jnp.float32
BF16 = jnp.bfloat16
EDGE = 16
LANES = 128
SUB = 384
PARAMS = pltpu.CompilerParams(vmem_limit_bytes=56 << 20)


def shape(dims, dtype):
    return jax.ShapeDtypeStruct(dims, dtype)


def dot(a, b):
    return jnp.dot(a, b, preferred_element_type=F32)


def dot_rows(a, b):
    return lax.dot_general(a, b, (((0,), (0,)), ((), ())), preferred_element_type=F32)


def dot_last(a, b):
    return lax.dot_general(a, b, (((1,), (1,)), ((), ())), preferred_element_type=F32)


def sigmoid(value):
    return 0.5 + 0.5 * jnp.tanh(0.5 * value)


def fill_padded(scratch, before, own, after):
    rows = own.shape[0]
    scratch[0:EDGE, :] = before[...].astype(F32)
    scratch[EDGE : EDGE + rows, :] = own[...].astype(F32)
    scratch[EDGE + rows : 2 * EDGE + rows, :] = after[...].astype(F32)


def conv_forward(before, own, after, segments, ids, weight, point, place):
    rows, width = own.shape
    length = segments.shape[1]
    taps = weight.shape[0]
    shift = EDGE - (taps - 1) // 2
    tall = rows + 2 * EDGE

    def kernel(
        place,
        before,
        own,
        after,
        segments,
        ids,
        weight,
        point,
        conv_out,
        act_out,
        packet,
        seg,
        scratch,
    ):
        fill_padded(scratch, before, own, after)
        frame = lax.broadcasted_iota(jnp.int32, (tall, length), 0) + (place[0] * rows - EDGE)
        chosen = frame == lax.broadcasted_iota(jnp.int32, (tall, length), 1)
        chosen = jnp.where(chosen, 1.0, 0.0).astype(BF16)
        numbers = jnp.broadcast_to(segments[...].astype(F32) + 1.0, (LANES, length))
        seg[...] = dot_last(chosen, numbers.astype(BF16)) - 1.0
        low = jnp.concatenate([ids[...].astype(F32), jnp.zeros((EDGE - 2, rows), F32)], axis=0)
        packet[rows:, :] = jnp.zeros((EDGE, width), BF16)
        packet[rows:, 0:rows] = low.astype(BF16)

        def column(index, carry):
            lanes = pl.ds(pl.multiple_of(index * LANES, LANES), LANES)
            seg_own = seg[EDGE : EDGE + rows, :]
            total = jnp.zeros((rows, LANES), F32)
            for tap in range(taps):
                first = tap + shift
                same = seg[first : first + rows, :] == seg_own
                piece = jnp.where(same, scratch[first : first + rows, lanes], 0.0)
                total = total + weight[tap : tap + 1, lanes] * piece
            conv_out[:, lanes] = total
            act_out[:, lanes] = (total * sigmoid(total)).astype(BF16)
            return carry

        lax.fori_loop(0, width // LANES, column, 0)
        packet[:rows, :] = (own[...].astype(F32) + dot(act_out[...], point[...])).astype(BF16)

    return pl.pallas_call(
        kernel,
        in_specs=[pl.BlockSpec(memory_space=pltpu.SMEM)]
        + [pl.BlockSpec(memory_space=pltpu.VMEM)] * 7,
        out_shape=(
            shape((rows, width), F32),
            shape((rows, width), BF16),
            shape((rows + EDGE, width), BF16),
            shape((tall, LANES), F32),
        ),
        scratch_shapes=[pltpu.VMEM((tall, width), F32)],
        compiler_params=PARAMS,
        name="conv_forward",
    )(place, before, own, after, segments, ids, weight, point)


def conv_backward_kernel(before, own, after, seg, weight, grad_mixed, out, scratch):
    rows, width = own.shape
    taps = weight.shape[0]
    shift = EDGE - (taps - 1) // 2
    fill_padded(scratch, before, own, after)

    def column(index, carry):
        lanes = pl.ds(pl.multiple_of(index * LANES, LANES), LANES)
        seg_own = seg[EDGE : EDGE + rows, :]
        total = grad_mixed[:, lanes]
        for tap in range(taps):
            first = tap + shift
            same = seg[first : first + rows, :] == seg_own
            piece = jnp.where(same, scratch[first : first + rows, lanes], 0.0)
            total = total + weight[taps - 1 - tap : taps - tap, lanes] * piece
        out[:, lanes] = total.astype(BF16)
        return carry

    lax.fori_loop(0, width // LANES, column, 0)


def conv_backward(before, own, after, seg, weight, grad_mixed):
    rows, width = own.shape
    return pl.pallas_call(
        conv_backward_kernel,
        out_shape=shape((rows, width), BF16),
        scratch_shapes=[pltpu.VMEM((rows + 2 * EDGE, width), F32)],
        compiler_params=PARAMS,
        name="conv_backward",
    )(before, own, after, seg, weight, grad_mixed)


def tail(
    where, parts, cot, conv, act, point_t, before, own, after, seg, router_part, places, taps, experts
):
    rows, width = own.shape
    shift = EDGE - (taps - 1) // 2
    groups = places // 2
    used = width // places
    lead = -(-used // EDGE) * EDGE
    extra = -(-(taps + 1 + experts) // EDGE)
    count = len(parts)
    pieces = (groups, lead + EDGE, width)

    def kernel(where, *refs):
        parts = refs[:count]
        cot, conv, act, point_t, before, own, after, seg, router_part = refs[count : count + 9]
        grad_mixed, grad_conv, mine, theirs, scratch, shared = refs[count + 9 :]
        core = where[0] % 2
        total = cot[...].astype(F32)
        for part in parts:
            total = total + part[...].astype(F32)
        grad_mixed[...] = total
        low = total.astype(BF16)
        grad_act = dot(low, point_t[...])
        value = conv[...]
        sigma = sigmoid(value)
        grad_conv[...] = (grad_act * (sigma * (1.0 + value * (1.0 - sigma)))).astype(BF16)
        fill_padded(scratch, before, own, after)
        point = dot_rows(act[...], low).astype(BF16)
        for index in range(places):
            side, group = divmod(index, groups)
            shared[side, group] = jnp.zeros(pieces[1:], BF16)
            shared[side, group, 0:used, :] = point[index * used : (index + 1) * used]

        def column(index, carry):
            lanes = pl.ds(pl.multiple_of(index * LANES, LANES), LANES)
            seg_own = seg[EDGE : EDGE + rows, :]
            slope = grad_conv[:, lanes].astype(F32)
            sums = []
            for tap in range(taps):
                first = tap + shift
                same = seg[first : first + rows, :] == seg_own
                piece = jnp.where(same, scratch[first : first + rows, lanes], 0.0)
                sums.append(jnp.sum(slope * piece, axis=0, keepdims=True))
            sums.append(jnp.zeros((1, LANES), F32))
            spot = lax.broadcasted_iota(jnp.int32, (experts, LANES), 0) == where[0]
            sums.append(jnp.where(spot, router_part[0:1, lanes], 0.0))
            missing = extra * EDGE - (taps + 1 + experts)
            if missing:
                sums.append(jnp.zeros((missing, LANES), F32))
            small = jnp.concatenate(sums, axis=0).astype(BF16)
            for index in range(extra):
                side, group = divmod(index, groups)
                shared[side, group, lead : lead + EDGE, lanes] = small[
                    index * EDGE : (index + 1) * EDGE
                ]
            return carry

        lax.fori_loop(0, width // LANES, column, 0)
        mine[...] = shared[core]
        theirs[...] = shared[1 - core]

    return pl.pallas_call(
        kernel,
        in_specs=[pl.BlockSpec(memory_space=pltpu.SMEM)]
        + [pl.BlockSpec(memory_space=pltpu.VMEM)] * (count + 9),
        out_shape=(
            shape((rows, width), F32),
            shape((rows, width), BF16),
            shape(pieces, BF16),
            shape(pieces, BF16),
        ),
        scratch_shapes=[
            pltpu.VMEM((rows + 2 * EDGE, width), F32),
            pltpu.VMEM((2,) + pieces, BF16),
        ],
        compiler_params=PARAMS,
        name="tail",
    )(where, *parts, cot, conv, act, point_t, before, own, after, seg, router_part)


def table_of(ids, experts, capacity):
    rows = ids.shape[1]
    ids = ids[0:2, :].astype(F32)
    expert = lax.broadcasted_iota(jnp.int32, (experts, rows), 0).astype(F32)
    named = [jnp.where(expert == ids[j : j + 1, :], 1.0, 0.0) for j in range(2)]
    earlier = lax.broadcasted_iota(jnp.int32, (rows, rows), 0)
    earlier = earlier < lax.broadcasted_iota(jnp.int32, (rows, rows), 1)
    counts = dot((named[0] + named[1]).astype(BF16), jnp.where(earlier, 1.0, 0.0).astype(BF16))
    row = lax.broadcasted_iota(jnp.int32, (experts * capacity, rows), 0).astype(F32)
    table = jnp.zeros((experts * capacity, rows), F32)
    for j in range(2):
        slot = jnp.sum(named[j] * counts, axis=0, keepdims=True)
        table = jnp.where(row == ids[j : j + 1, :] * capacity + slot, 1.0, table)
    return table.astype(BF16)


def place_own(packet, cot, experts, capacity):
    rows, width = cot.shape

    def kernel(packet, cot, out, table_out):
        table = table_of(packet[rows:, :rows], experts, capacity)
        table_out[...] = table
        for index, array in enumerate((packet[:rows, :], cot[...])):
            placed = dot(table, array).astype(BF16)
            for expert in range(experts):
                start = (2 * expert + index) * capacity
                piece = placed[expert * capacity : (expert + 1) * capacity]
                out[start : start + capacity, :] = piece

    return pl.pallas_call(
        kernel,
        out_shape=(
            shape((2 * experts * capacity, width), BF16),
            shape((experts * capacity, rows), BF16),
        ),
        compiler_params=PARAMS,
        name="place_own",
    )(packet, cot)


def place_rest(packets, experts, capacity):
    count = len(packets)
    rows, width = packets[0].shape[0] - EDGE, packets[0].shape[1]
    per_expert = count * capacity

    def kernel(*refs):
        out, tables = refs[count:]
        for k, packet in enumerate(refs[:count]):
            table = table_of(packet[rows:, :rows], experts, capacity)
            tables[k] = table
            placed = dot(table, packet[:rows, :]).astype(BF16)
            for expert in range(experts):
                start = expert * per_expert + k * capacity
                piece = placed[expert * capacity : (expert + 1) * capacity]
                out[start : start + capacity, :] = piece

    return pl.pallas_call(
        kernel,
        out_shape=(
            shape((experts * per_expert, width), BF16),
            shape((count, experts * capacity, rows), BF16),
        ),
        compiler_params=PARAMS,
        name="place_rest",
    )(*packets)


def place_more(tables, arrays, experts, capacity):
    count, _, rows = tables.shape
    width = arrays[0].shape[1]
    per_expert = count * capacity

    def kernel(tables, *refs):
        out = refs[count]
        for k, array in enumerate(refs[:count]):
            placed = dot(tables[k], array[...]).astype(BF16)
            for expert in range(experts):
                start = expert * per_expert + k * capacity
                piece = placed[expert * capacity : (expert + 1) * capacity]
                out[start : start + capacity, :] = piece

    return pl.pallas_call(
        kernel,
        out_shape=shape((experts * per_expert, width), BF16),
        compiler_params=PARAMS,
        name="place_more",
    )(tables, *arrays)


def collect(table, tables, buffer, experts, capacity):
    rest, _, rows = tables.shape
    count = rest + 1
    width = buffer.shape[1]
    per_expert = count * capacity

    def kernel(table, tables, buffer, *outs):
        for k, out in enumerate(outs):
            starts = [expert * per_expert + k * capacity for expert in range(experts)]
            pieces = [buffer[start : start + capacity, :] for start in starts]
            here = tables[k - 1] if k else table[...]
            out[...] = dot_rows(here, jnp.concatenate(pieces, axis=0)).astype(BF16)

    return pl.pallas_call(
        kernel,
        out_shape=[shape((rows, width), BF16)] * count,
        compiler_params=PARAMS,
        name="collect",
    )(table, tables, buffer)


def expert_specs(own, rest):
    places, _, capacity, width = own.shape
    packs = rest.shape[1] + 1
    group = max(1, SUB // (packs * capacity))
    chunk = group * packs * capacity

    def by_place(*dims):
        zeros = (0,) * len(dims)
        return pl.BlockSpec((group,) + dims, lambda i: (i,) + zeros)

    def flat(columns):
        return pl.BlockSpec((chunk, columns), lambda i: (i, 0))

    def full(dims):
        return pl.BlockSpec(dims, lambda i: (0,) * len(dims))

    return packs, group, chunk, by_place, flat, full


def by_cell(own, rest, which, group):
    pieces = []
    for place in range(group):
        pieces.append(own[place, which])
        pieces += [rest[place, k] for k in range(rest.shape[1])]
    return jnp.concatenate(pieces, axis=0)


def chosen_expert(where, rows, columns, axis):
    index = lax.broadcasted_iota(jnp.int32, (rows, columns), axis)
    return jnp.where(index == where[0], 1.0, 0.0).astype(BF16)


def expert_forward(where, own, rest, weight_in, weight_out, router_weight):
    places, _, capacity, width = own.shape
    inner = weight_in.shape[1]
    packs, group, chunk, by_place, flat, full = expert_specs(own, rest)
    total = places * packs * capacity

    experts = router_weight.shape[0]

    def kernel(where, own, rest, w_in, w_out, router, *outs):
        gated_out, rows_out, hidden_out, slope_out, gate_out = outs
        row = by_cell(own, rest, 0, group)
        rows_out[...] = row
        router_rows = dot(chosen_expert(where, LANES, experts, 1), router[...]).astype(BF16)
        gate = sigmoid(dot_last(row, router_rows))
        gate_out[...] = gate
        pre = dot(row, w_in[...])
        sigma = sigmoid(pre)
        hidden = (pre * sigma).astype(BF16)
        hidden_out[...] = hidden
        slope_out[...] = (sigma * (1.0 + pre * (1.0 - sigma))).astype(BF16)
        gate_wide = jnp.concatenate([gate] * (width // LANES), axis=1)
        gated = (gate_wide * dot(hidden, w_out[...])).astype(BF16)
        gated_out[...] = gated.reshape(gated_out.shape)

    return pl.pallas_call(
        kernel,
        grid=(places // group,),
        in_specs=[
            pl.BlockSpec(memory_space=pltpu.SMEM),
            by_place(2, capacity, width),
            by_place(packs - 1, capacity, width),
            full(weight_in.shape),
            full(weight_out.shape),
            full(router_weight.shape),
        ],
        out_specs=[by_place(packs * capacity, width)]
        + [flat(width), flat(inner), flat(inner), flat(LANES)],
        out_shape=[
            shape((places, packs * capacity, width), BF16),
            shape((total, width), BF16),
            shape((total, inner), BF16),
            shape((total, inner), BF16),
            shape((total, LANES), F32),
        ],
        compiler_params=PARAMS,
        name="expert_forward",
    )(where, own, rest, weight_in, weight_out, router_weight)


def expert_backward(
    where, rows, own, rest, gated, slope, gate, weight_in_t, weight_out_t, router_weight
):
    places, _, capacity, width = own.shape
    inner = weight_in_t.shape[0]
    packs, group, chunk, by_place, flat, full = expert_specs(own, rest)
    total = places * packs * capacity

    experts = router_weight.shape[0]

    def kernel(where, rows, own, rest, gated, slope, gate, w_in_t, w_out_t, router, *outs):
        back_out, grad_pre_out, grad_y_out, router_out = outs
        cot = by_cell(own, rest, 1, group).astype(F32)
        gates = gate[...]
        gate_wide = jnp.concatenate([gates] * (width // LANES), axis=1)
        grad_y = (gate_wide * cot).astype(BF16)
        grad_y_out[...] = grad_y
        grad_pre = (dot(grad_y, w_out_t[...]) * slope[...].astype(F32)).astype(BF16)
        grad_pre_out[...] = grad_pre
        out = gated[...].reshape(chunk, width).astype(F32)
        grad_gate = jnp.sum(cot * out, axis=1, keepdims=True)
        grad_logit = grad_gate * (1.0 - gates)[:, 0:1]
        router_row = dot(chosen_expert(where, 8, experts, 1), router[...])[0:1, :]
        back = dot(grad_pre, w_in_t[...]) + grad_logit * router_row
        back_out[...] = back.astype(BF16).reshape(back_out.shape)
        partial = jnp.sum(rows[...].astype(F32) * grad_logit, axis=0, keepdims=True)

        @pl.when(pl.program_id(0) == 0)
        def _():
            router_out[...] = jnp.zeros_like(router_out)

        router_out[0:1, :] += partial

    return pl.pallas_call(
        kernel,
        grid=(places // group,),
        in_specs=[
            pl.BlockSpec(memory_space=pltpu.SMEM),
            flat(width),
            by_place(2, capacity, width),
            by_place(packs - 1, capacity, width),
            by_place(packs * capacity, width),
            flat(inner),
            flat(LANES),
            full(weight_in_t.shape),
            full(weight_out_t.shape),
            full(router_weight.shape),
        ],
        out_specs=(
            by_place(packs * capacity, width),
            flat(inner),
            flat(width),
            full((8, width)),
        ),
        out_shape=(
            shape((places, packs * capacity, width), BF16),
            shape((total, inner), BF16),
            shape((total, width), BF16),
            shape((8, width), F32),
        ),
        compiler_params=PARAMS,
        name="expert_backward",
    )(where, rows, own, rest, gated, slope, gate, weight_in_t, weight_out_t, router_weight)


def add_pieces(mine, theirs, group):
    groups, size, width = mine.shape

    def kernel(group, mine, theirs, *outs):
        for index, out in enumerate(outs):
            here = group[0] ^ index
            out[...] = (mine[here].astype(F32) + theirs[here].astype(F32)).astype(BF16)

    return pl.pallas_call(
        kernel,
        in_specs=[pl.BlockSpec(memory_space=pltpu.SMEM)]
        + [pl.BlockSpec(memory_space=pltpu.VMEM)] * 2,
        out_shape=[shape((size, width), BF16)] * groups,
        compiler_params=PARAMS,
        name="add_pieces",
    )(group, mine, theirs)


def spread(own, other, group, core, used, taps, experts):
    count = len(own)
    size, width = own[0].shape

    def kernel(where, *refs):
        point, conv, router, small = refs[2 * count :]
        for index in range(2 * count):
            side = where[1] if index < count else 1 - where[1]
            place = side * count + (where[0] ^ (index % count))
            piece = refs[index][...].astype(F32)
            point[pl.ds(pl.multiple_of(place * used, 8), used), :] = piece[:used]
            small[place] = piece[size - EDGE :]
        last = -(-(taps + 1 + experts) // EDGE)
        rows = jnp.concatenate([small[place] for place in range(last)], axis=0)
        conv[...] = rows[:taps]
        router[...] = rows[taps + 1 : taps + 1 + experts]

    return pl.pallas_call(
        kernel,
        in_specs=[pl.BlockSpec(memory_space=pltpu.SMEM)]
        + [pl.BlockSpec(memory_space=pltpu.VMEM)] * (2 * count),
        out_shape=(
            shape((2 * count * used, width), F32),
            shape((taps, width), F32),
            shape((experts, width), F32),
        ),
        scratch_shapes=[pltpu.VMEM((2 * count, EDGE, width), F32)],
        compiler_params=PARAMS,
        name="spread",
    )(jnp.stack([group, core]), *own, *other)


def swap(array, axis, k):
    devices = lax.axis_size(axis)
    return lax.ppermute(array, axis, [(i, i ^ k) for i in range(devices)])


def from_all(array, axis):
    return [array] + [swap(array, axis, k) for k in range(1, lax.axis_size(axis))]


def to_all(arrays, axis):
    return [part if k == 0 else swap(part, axis, k) for k, part in enumerate(arrays)]


def exchange(array, axis):
    return lax.all_to_all(array, axis, split_axis=0, concat_axis=0, tiled=True)


def after_all(array, others):
    return lax.optimization_barrier((array, tuple(others)))[0]


def edges(array, axis):
    devices = lax.axis_size(axis)
    up = [(i, i + 1) for i in range(devices - 1)]
    down = [(j, i) for i, j in up]
    before = lax.ppermute(array[array.shape[0] - EDGE :], axis, up)
    after = lax.ppermute(array[:EDGE], axis, down)
    return before, after


def sum_parts(parts):
    parts = [part.astype(F32) for part in parts]
    while len(parts) > 1:
        parts = [a + b for a, b in zip(parts[::2], parts[1::2])]
    return parts[0]


def local(
    frames,
    segments,
    conv_weight,
    point_weight,
    router_weight,
    expert_ids,
    expert_in,
    expert_out,
    cotangent,
):
    rows_here, width = frames.shape[1:]
    taps = conv_weight.shape[0]
    experts = router_weight.shape[1]
    capacity = -(-3 * rows_here // experts // EDGE) * EDGE
    packs = lax.axis_size("dp")
    places = lax.axis_size("seq")
    place_here = lax.axis_index("seq")
    own_frames = frames[0]
    own_cot = cotangent[0]
    before, after = edges(own_frames, "seq")

    where = place_here[None]
    conv, activated, packet, seg = conv_forward(
        before, own_frames, after, segments, expert_ids[0].T, conv_weight, point_weight, where
    )
    packets = from_all(packet, "dp")
    cell = (places, -1, capacity, width)

    own_placed, table = place_own(packet, own_cot, experts, capacity)
    own_rows = exchange(own_placed.reshape(places, -1, width), "seq").reshape(cell)
    rest_placed, tables = place_rest(packets[1:], experts, capacity)
    cots = from_all(after_all(own_cot, packets), "dp")
    rest_placed, own_rows, cots[1] = lax.optimization_barrier((rest_placed, own_rows, cots[1]))
    rest_rows = exchange(rest_placed.reshape(places, -1, width), "seq")
    cots_placed = place_more(tables, cots[1:], experts, capacity)
    cots_placed, rest_rows = lax.optimization_barrier((cots_placed, rest_rows))
    rest_cots = exchange(cots_placed.reshape(places, -1, width), "seq").reshape(cell)
    rest_rows = rest_rows.reshape(cell)

    weight_in = expert_in[0]
    weight_out = expert_out[0]
    gated, rows, hidden, slope, gate = expert_forward(
        where, own_rows, rest_rows, weight_in, weight_out, router_weight.T
    )
    weight_in, weight_out, gated = lax.optimization_barrier((weight_in, weight_out, gated))
    back, grad_pre, grad_y, router_part = expert_backward(
        where,
        rows,
        own_rows,
        rest_cots,
        gated,
        slope,
        gate,
        weight_in.T,
        weight_out.T,
        router_weight.T,
    )
    back_home = exchange(back, "seq")
    grad_wout = dot_rows(hidden, grad_y)
    grad_win = dot_rows(rows, grad_pre)
    point_t = after_all(point_weight, (back,)).T
    back_home, grad_wout, grad_win, point_t = lax.optimization_barrier(
        (back_home, grad_wout, grad_win, point_t)
    )
    back_parts = collect(table, tables, back_home.reshape(-1, width), experts, capacity)
    gated_home = exchange(after_all(gated, back_parts), "seq")
    back_own = to_all(back_parts, "dp")

    core = place_here % 2
    group = place_here // 2
    groups = places // 2
    grad_mixed, grad_conv, mine, theirs = tail(
        where,
        back_own,
        own_cot,
        conv,
        activated,
        point_t,
        before,
        own_frames,
        after,
        seg,
        router_part,
        places,
        taps,
        experts,
    )
    pieces = add_pieces(mine, swap(theirs, "seq", 1), group[None])
    pieces = [pieces[0]] + [swap(pieces[m], "seq", 2 * m) for m in range(1, groups)]
    gated_parts = collect(table, tables, gated_home.reshape(-1, width), experts, capacity)
    pieces, gated_parts = lax.optimization_barrier((pieces, gated_parts))
    share = sum_parts(pieces).astype(BF16)
    grad_before, grad_after = edges(grad_conv, "seq")
    frames_grad = conv_backward(grad_before, grad_conv, grad_after, seg, conv_weight, grad_mixed)
    share = sum_parts(from_all(share, "dp")).astype(BF16)
    share, frames_grad, gated_parts = lax.optimization_barrier((share, frames_grad, gated_parts))
    gated_own = to_all(gated_parts, "dp")
    block_out = (packet[:rows_here].astype(F32) + sum_parts(gated_own)).astype(BF16)
    own_half = [share] + [swap(share, "seq", 2 * m) for m in range(1, groups)]
    other_half = [swap(part, "seq", 1) for part in own_half]
    point_grad, conv_grad, router_rows = spread(
        own_half, other_half, group, core, width // places, taps, experts
    )
    router_grad = router_rows.T
    return (
        block_out[None],
        frames_grad[None],
        conv_grad,
        router_grad,
        point_grad,
        grad_win[None],
        grad_wout[None],
    )


def solution(mesh):
    placed = (
        P("dp", "seq", None),
        P("dp", None),
        P(),
        P(),
        P(),
        P("dp", "seq", None),
        P("seq", None, "dp"),
        P("seq", "dp", None),
        P("dp", "seq", None),
    )
    return jax.shard_map(
        local,
        mesh=mesh,
        in_specs=placed,
        out_specs=(
            P("dp", "seq", None),
            P("dp", "seq", None),
            P(),
            P(),
            P(),
            P("seq", None, "dp"),
            P("seq", "dp", None),
        ),
        check_vma=False,
    )
```

```python
import jax
import jax.numpy as jnp
from jax import lax
from jax.experimental import pallas as pl
from jax.experimental.pallas import tpu as pltpu
from jax.sharding import PartitionSpec as P

F32 = jnp.float32
BF16 = jnp.bfloat16
EDGE = 16
LANES = 128
SUB = 384
PARAMS = pltpu.CompilerParams(vmem_limit_bytes=56 << 20)


def shape(dims, dtype):
    return jax.ShapeDtypeStruct(dims, dtype)


def dot(a, b):
    return jnp.dot(a, b, preferred_element_type=F32)


def dot_rows(a, b):
    return lax.dot_general(a, b, (((0,), (0,)), ((), ())), preferred_element_type=F32)


def dot_last(a, b):
    return lax.dot_general(a, b, (((1,), (1,)), ((), ())), preferred_element_type=F32)


def sigmoid(value):
    return 0.5 + 0.5 * jnp.tanh(0.5 * value)


def fill_padded(scratch, before, own, after):
    rows = own.shape[0]
    scratch[0:EDGE, :] = before[...].astype(F32)
    scratch[EDGE : EDGE + rows, :] = own[...].astype(F32)
    scratch[EDGE + rows : 2 * EDGE + rows, :] = after[...].astype(F32)


def conv_forward(before, own, after, segments, weight, point, place):
    rows, width = own.shape
    length = segments.shape[1]
    taps = weight.shape[0]
    shift = EDGE - (taps - 1) // 2
    tall = rows + 2 * EDGE

    def kernel(
        place,
        before,
        own,
        after,
        segments,
        weight,
        point,
        conv_out,
        act_out,
        mixed,
        seg,
        scratch,
    ):
        fill_padded(scratch, before, own, after)
        frame = lax.broadcasted_iota(jnp.int32, (tall, length), 0) + (place[0] * rows - EDGE)
        chosen = frame == lax.broadcasted_iota(jnp.int32, (tall, length), 1)
        chosen = jnp.where(chosen, 1.0, 0.0).astype(BF16)
        numbers = jnp.broadcast_to(segments[...].astype(F32) + 1.0, (LANES, length))
        seg[...] = dot_last(chosen, numbers.astype(BF16)) - 1.0

        def column(index, carry):
            lanes = pl.ds(pl.multiple_of(index * LANES, LANES), LANES)
            seg_own = seg[EDGE : EDGE + rows, :]
            total = jnp.zeros((rows, LANES), F32)
            for tap in range(taps):
                first = tap + shift
                same = seg[first : first + rows, :] == seg_own
                piece = jnp.where(same, scratch[first : first + rows, lanes], 0.0)
                total = total + weight[tap : tap + 1, lanes] * piece
            conv_out[:, lanes] = total
            act_out[:, lanes] = (total * sigmoid(total)).astype(BF16)
            return carry

        lax.fori_loop(0, width // LANES, column, 0)
        mixed[...] = (own[...].astype(F32) + dot(act_out[...], point[...])).astype(BF16)

    return pl.pallas_call(
        kernel,
        in_specs=[pl.BlockSpec(memory_space=pltpu.SMEM)]
        + [pl.BlockSpec(memory_space=pltpu.VMEM)] * 6,
        out_shape=(
            shape((rows, width), F32),
            shape((rows, width), BF16),
            shape((rows, width), BF16),
            shape((tall, LANES), F32),
        ),
        scratch_shapes=[pltpu.VMEM((tall, width), F32)],
        compiler_params=PARAMS,
        name="conv_forward",
    )(place, before, own, after, segments, weight, point)


def conv_backward_kernel(before, own, after, seg, weight, grad_mixed, out, scratch):
    rows, width = own.shape
    taps = weight.shape[0]
    shift = EDGE - (taps - 1) // 2
    fill_padded(scratch, before, own, after)

    def column(index, carry):
        lanes = pl.ds(pl.multiple_of(index * LANES, LANES), LANES)
        seg_own = seg[EDGE : EDGE + rows, :]
        total = grad_mixed[:, lanes]
        for tap in range(taps):
            first = tap + shift
            same = seg[first : first + rows, :] == seg_own
            piece = jnp.where(same, scratch[first : first + rows, lanes], 0.0)
            total = total + weight[taps - 1 - tap : taps - tap, lanes] * piece
        out[:, lanes] = total.astype(BF16)
        return carry

    lax.fori_loop(0, width // LANES, column, 0)


def conv_backward(before, own, after, seg, weight, grad_mixed):
    rows, width = own.shape
    return pl.pallas_call(
        conv_backward_kernel,
        out_shape=shape((rows, width), BF16),
        scratch_shapes=[pltpu.VMEM((rows + 2 * EDGE, width), F32)],
        compiler_params=PARAMS,
        name="conv_backward",
    )(before, own, after, seg, weight, grad_mixed)


def tail(
    where, parts, cot, conv, act, point_w, before, own, after, seg, router_part, places, taps, experts
):
    rows, width = own.shape
    shift = EDGE - (taps - 1) // 2
    groups = places // 2
    used = width // places
    lead = -(-used // EDGE) * EDGE
    extra = -(-(taps + 1 + experts) // EDGE)
    count = len(parts)
    pieces = (groups, lead + EDGE, width)

    def kernel(where, *refs):
        parts = refs[:count]
        cot, conv, act, point_w, before, own, after, seg, router_part = refs[count : count + 9]
        grad_mixed, grad_conv, mine, theirs, scratch, shared = refs[count + 9 :]
        core = where[0] % 2
        total = cot[...].astype(F32)
        for part in parts:
            total = total + part[...].astype(F32)
        grad_mixed[...] = total
        low = total.astype(BF16)
        grad_act = dot_last(low, point_w[...])
        value = conv[...]
        sigma = sigmoid(value)
        grad_conv[...] = (grad_act * (sigma * (1.0 + value * (1.0 - sigma)))).astype(BF16)
        fill_padded(scratch, before, own, after)
        point = dot_rows(act[...], low).astype(BF16)
        for index in range(places):
            side, group = divmod(index, groups)
            shared[side, group] = jnp.zeros(pieces[1:], BF16)
            shared[side, group, 0:used, :] = point[index * used : (index + 1) * used]

        def column(index, carry):
            lanes = pl.ds(pl.multiple_of(index * LANES, LANES), LANES)
            seg_own = seg[EDGE : EDGE + rows, :]
            slope = grad_conv[:, lanes].astype(F32)
            sums = []
            for tap in range(taps):
                first = tap + shift
                same = seg[first : first + rows, :] == seg_own
                piece = jnp.where(same, scratch[first : first + rows, lanes], 0.0)
                sums.append(jnp.sum(slope * piece, axis=0, keepdims=True))
            sums.append(jnp.zeros((1, LANES), F32))
            spot = lax.broadcasted_iota(jnp.int32, (experts, LANES), 0) == where[0]
            sums.append(jnp.where(spot, router_part[0:1, lanes], 0.0))
            missing = extra * EDGE - (taps + 1 + experts)
            if missing:
                sums.append(jnp.zeros((missing, LANES), F32))
            small = jnp.concatenate(sums, axis=0).astype(BF16)
            for index in range(extra):
                side, group = divmod(index, groups)
                shared[side, group, lead : lead + EDGE, lanes] = small[
                    index * EDGE : (index + 1) * EDGE
                ]
            return carry

        lax.fori_loop(0, width // LANES, column, 0)
        mine[...] = shared[core]
        theirs[...] = shared[1 - core]

    return pl.pallas_call(
        kernel,
        in_specs=[pl.BlockSpec(memory_space=pltpu.SMEM)]
        + [pl.BlockSpec(memory_space=pltpu.VMEM)] * (count + 9),
        out_shape=(
            shape((rows, width), F32),
            shape((rows, width), BF16),
            shape(pieces, BF16),
            shape(pieces, BF16),
        ),
        scratch_shapes=[
            pltpu.VMEM((rows + 2 * EDGE, width), F32),
            pltpu.VMEM((2,) + pieces, BF16),
        ],
        compiler_params=PARAMS,
        name="tail",
    )(where, *parts, cot, conv, act, point_w, before, own, after, seg, router_part)


def table_of(ids, experts, capacity):
    rows = ids.shape[1]
    ids = ids[0:2, :].astype(F32)
    expert = lax.broadcasted_iota(jnp.int32, (experts, rows), 0).astype(F32)
    named = [jnp.where(expert == ids[j : j + 1, :], 1.0, 0.0) for j in range(2)]
    earlier = lax.broadcasted_iota(jnp.int32, (rows, rows), 0)
    earlier = earlier < lax.broadcasted_iota(jnp.int32, (rows, rows), 1)
    counts = dot((named[0] + named[1]).astype(BF16), jnp.where(earlier, 1.0, 0.0).astype(BF16))
    row = lax.broadcasted_iota(jnp.int32, (experts * capacity, rows), 0).astype(F32)
    table = jnp.zeros((experts * capacity, rows), F32)
    for j in range(2):
        slot = jnp.sum(named[j] * counts, axis=0, keepdims=True)
        table = jnp.where(row == ids[j : j + 1, :] * capacity + slot, 1.0, table)
    return table.astype(BF16)


def place_packets(packets, experts, capacity):
    count = len(packets)
    rows, width = packets[0].shape[0] - EDGE, packets[0].shape[1]
    per_expert = count * capacity

    def kernel(*refs):
        out, tables = refs[count:]
        for k, packet in enumerate(refs[:count]):
            table = table_of(packet[rows:, :rows], experts, capacity)
            tables[k] = table
            placed = dot(table, packet[:rows, :]).astype(BF16)
            for expert in range(experts):
                start = expert * per_expert + k * capacity
                piece = placed[expert * capacity : (expert + 1) * capacity]
                out[start : start + capacity, :] = piece

    return pl.pallas_call(
        kernel,
        out_shape=(
            shape((experts * per_expert, width), BF16),
            shape((count, experts * capacity, rows), BF16),
        ),
        compiler_params=PARAMS,
        name="place_packets",
    )(*packets)


def split_tables(refs, counts):
    return [ref.at[k] for ref, count in zip(refs, counts) for k in range(count)]


def place_rows(where, tables, arrays, experts, capacity):
    counts = [table.shape[0] for table in tables]
    groups = len(tables)
    width = arrays[0].shape[1]
    per_expert = len(arrays) * capacity
    given = groups + len(arrays)

    def kernel(where, *refs):
        outs, scratch = refs[given:-1], refs[-1]
        here = split_tables(refs[:groups], counts)
        for k, (table, array) in enumerate(zip(here, refs[groups:given])):
            placed = dot(table[...], array[...]).astype(BF16)
            for expert in range(experts):
                piece = placed[expert * capacity : (expert + 1) * capacity]
                scratch[expert, k * capacity : (k + 1) * capacity, :] = piece
        for index, out in enumerate(outs):
            out[...] = scratch[where[0] ^ index]

    return pl.pallas_call(
        kernel,
        in_specs=[pl.BlockSpec(memory_space=pltpu.SMEM)]
        + [pl.BlockSpec(memory_space=pltpu.VMEM)] * given,
        out_shape=[shape((per_expert, width), BF16)] * experts,
        scratch_shapes=[pltpu.VMEM((experts, per_expert, width), BF16)],
        compiler_params=PARAMS,
        name="place_rows",
    )(where, *tables, *arrays)


def collect(tables, buffer, experts, capacity):
    counts = [table.shape[0] for table in tables]
    groups = len(tables)
    rows = tables[0].shape[2]
    width = buffer.shape[1]
    per_expert = sum(counts) * capacity

    def kernel(*refs):
        buffer = refs[groups]
        here = split_tables(refs[:groups], counts)
        for k, (table, out) in enumerate(zip(here, refs[groups + 1 :])):
            starts = [expert * per_expert + k * capacity for expert in range(experts)]
            pieces = [buffer[start : start + capacity, :] for start in starts]
            out[...] = dot_rows(table[...], jnp.concatenate(pieces, axis=0)).astype(BF16)

    return pl.pallas_call(
        kernel,
        out_shape=[shape((rows, width), BF16)] * sum(counts),
        compiler_params=PARAMS,
        name="collect",
    )(*tables, buffer)


def chosen_expert(where, rows, columns, axis):
    index = lax.broadcasted_iota(jnp.int32, (rows, columns), axis)
    return jnp.where(index == where[0], 1.0, 0.0).astype(BF16)


def collect_packs(pack_here, table, buffer, experts, capacity):
    count, _, rows = table.shape
    width = buffer.shape[1]
    per_expert = count * capacity

    def kernel(pack_here, table, buffer, out):
        for k in range(count):
            starts = [expert * per_expert + k * capacity for expert in range(experts)]
            pieces = [buffer[start : start + capacity, :] for start in starts]
            summed = dot_rows(table[k], jnp.concatenate(pieces, axis=0))
            out[pack_here[0] ^ k] = summed.astype(BF16)

    return pl.pallas_call(
        kernel,
        in_specs=[pl.BlockSpec(memory_space=pltpu.SMEM)]
        + [pl.BlockSpec(memory_space=pltpu.VMEM)] * 2,
        out_shape=shape((count, rows, width), BF16),
        compiler_params=PARAMS,
        name="collect_packs",
    )(pack_here, table, buffer)


def expert(where, rows, cots, weights, router_weight):
    places, packs, capacity, width = cots.shape
    inner = weights[0].shape[1]
    experts = router_weight.shape[0]
    per_place = packs * capacity
    total = places * per_place
    group = 1
    while 2 * group * per_place <= SUB and places % (2 * group) == 0:
        group = 2 * group
    chunk = group * per_place

    def kernel(where, *refs):
        rows = refs[:places]
        cots, w_in, w_out, router = refs[places : places + 4]
        back_out, gated_out, rows_out, hidden_out, grad_pre_out, grad_y_out, router_out = refs[
            places + 4 : -1
        ]
        scratch = refs[-1]
        step = pl.program_id(0)

        @pl.when(step == 0)
        def _():
            router_out[...] = jnp.zeros_like(router_out)
            for index, ref in enumerate(rows):
                scratch[index] = ref[...]

        inside = where[0] % group
        row = jnp.concatenate([scratch[step * group + index] for index in range(group)], axis=0)
        rows_out[...] = row
        cot = jnp.concatenate(
            [cots[inside ^ index].reshape(per_place, width) for index in range(group)], axis=0
        ).astype(F32)
        router_rows = dot(chosen_expert(where, LANES, experts, 1), router[...])
        gate = sigmoid(dot_last(row, router_rows.astype(BF16)))
        gate_wide = jnp.concatenate([gate] * (width // LANES), axis=1)
        grad_y = (gate_wide * cot).astype(BF16)
        grad_y_out[...] = grad_y
        pre = dot(row, w_in[...])
        sigma = sigmoid(pre)
        hidden = (pre * sigma).astype(BF16)
        hidden_out[...] = hidden
        slope = sigma * (1.0 + pre * (1.0 - sigma))
        grad_pre = (dot_last(grad_y, w_out[...]) * slope).astype(BF16)
        grad_pre_out[...] = grad_pre
        gated = gate_wide * dot(hidden, w_out[...])
        grad_gate = jnp.sum(cot * gated, axis=1, keepdims=True)
        grad_logit = grad_gate * (1.0 - gate)[:, 0:1]
        back = (dot_last(grad_pre, w_in[...]) + grad_logit * router_rows[0:1, :]).astype(BF16)
        gated = gated.astype(BF16)
        for index in range(group):
            piece = slice(index * per_place, (index + 1) * per_place)
            gated_out[inside ^ index] = gated[piece]
            back_out[inside ^ index] = back[piece]
        router_out[0:1, :] += jnp.sum(row.astype(F32) * grad_logit, axis=0, keepdims=True)

    def by_place(*dims):
        zeros = (0,) * len(dims)
        return pl.BlockSpec((group,) + dims, lambda i, where: (i ^ (where[0] // group),) + zeros)

    def flat(columns):
        return pl.BlockSpec((chunk, columns), lambda i, where: (i, 0))

    def full(dims):
        return pl.BlockSpec(dims, lambda i, where: (0,) * len(dims))

    return pl.pallas_call(
        kernel,
        grid_spec=pltpu.PrefetchScalarGridSpec(
            num_scalar_prefetch=1,
            grid=(places // group,),
            in_specs=[full((per_place, width))] * places
            + [by_place(packs, capacity, width)]
            + [full(weight.shape) for weight in weights]
            + [full(router_weight.shape)],
            out_specs=[
                by_place(per_place, width),
                by_place(per_place, width),
                flat(width),
                flat(inner),
                flat(inner),
                flat(width),
                full((8, width)),
            ],
            scratch_shapes=[pltpu.VMEM((places, per_place, width), BF16)],
        ),
        out_shape=[
            shape((places, per_place, width), BF16),
            shape((places, per_place, width), BF16),
            shape((total, width), BF16),
            shape((total, inner), BF16),
            shape((total, inner), BF16),
            shape((total, width), BF16),
            shape((8, width), F32),
        ],
        compiler_params=PARAMS,
        name="expert",
    )(where, *rows, cots, *weights, router_weight)


def add_pieces(mine, theirs, group):
    groups, size, width = mine.shape

    def kernel(group, mine, theirs, *outs):
        for index, out in enumerate(outs):
            here = group[0] ^ index
            out[...] = (mine[here].astype(F32) + theirs[here].astype(F32)).astype(BF16)

    return pl.pallas_call(
        kernel,
        in_specs=[pl.BlockSpec(memory_space=pltpu.SMEM)]
        + [pl.BlockSpec(memory_space=pltpu.VMEM)] * 2,
        out_shape=[shape((size, width), BF16)] * groups,
        compiler_params=PARAMS,
        name="add_pieces",
    )(group, mine, theirs)


def spread(own, other, group, core, used, taps, experts):
    count = len(own)
    size, width = own[0].shape

    def kernel(where, *refs):
        point, conv, router, small = refs[2 * count :]
        for index in range(2 * count):
            side = where[1] if index < count else 1 - where[1]
            place = side * count + (where[0] ^ (index % count))
            piece = refs[index][...].astype(F32)
            point[pl.ds(pl.multiple_of(place * used, 8), used), :] = piece[:used]
            small[place] = piece[size - EDGE :]
        last = -(-(taps + 1 + experts) // EDGE)
        rows = jnp.concatenate([small[place] for place in range(last)], axis=0)
        conv[...] = rows[:taps]
        router[...] = rows[taps + 1 : taps + 1 + experts]

    return pl.pallas_call(
        kernel,
        in_specs=[pl.BlockSpec(memory_space=pltpu.SMEM)]
        + [pl.BlockSpec(memory_space=pltpu.VMEM)] * (2 * count),
        out_shape=(
            shape((2 * count * used, width), F32),
            shape((taps, width), F32),
            shape((experts, width), F32),
        ),
        scratch_shapes=[pltpu.VMEM((2 * count, EDGE, width), F32)],
        compiler_params=PARAMS,
        name="spread",
    )(jnp.stack([group, core]), *own, *other)


def swap(array, axis, k):
    devices = lax.axis_size(axis)
    return lax.ppermute(array, axis, [(i, i ^ k) for i in range(devices)])


def from_all(array, axis):
    return [array] + [swap(array, axis, k) for k in range(1, lax.axis_size(axis))]


def to_all(arrays, axis):
    return [part if k == 0 else swap(part, axis, k) for k, part in enumerate(arrays)]


def exchange(array, axis):
    return lax.all_to_all(array, axis, split_axis=0, concat_axis=0, tiled=True)


def to_all_blocks(arrays, axis):
    count = len(arrays)
    if count <= 8:
        return to_all(arrays, axis)
    order = jnp.arange(count, dtype=jnp.int32) ^ lax.axis_index(axis)
    moved = exchange(jnp.stack(arrays)[order], axis)[order]
    return [moved[k] for k in range(count)]


def after_all(array, others):
    return lax.optimization_barrier((array, tuple(others)))[0]


def edges(array, axis):
    devices = lax.axis_size(axis)
    up = [(i, i + 1) for i in range(devices - 1)]
    down = [(j, i) for i, j in up]
    before = lax.ppermute(array[array.shape[0] - EDGE :], axis, up)
    after = lax.ppermute(array[:EDGE], axis, down)
    return before, after


def sum_parts(parts):
    parts = [part.astype(F32) for part in parts]
    while len(parts) > 1:
        parts = [a + b for a, b in zip(parts[::2], parts[1::2])]
    return parts[0]


def local(
    frames,
    segments,
    conv_weight,
    point_weight,
    router_weight,
    expert_ids,
    expert_in,
    expert_out,
    cotangent,
):
    rows_here, width = frames.shape[1:]
    taps = conv_weight.shape[0]
    experts = router_weight.shape[1]
    capacity = -(-3 * rows_here // experts // EDGE) * EDGE
    packs = lax.axis_size("dp")
    places = lax.axis_size("seq")
    place_here = lax.axis_index("seq")
    own_frames = frames[0]
    own_cot = cotangent[0]
    before, after = edges(own_frames, "seq")

    where = place_here[None]

    ids = jnp.pad(expert_ids[0].T.astype(BF16), ((0, EDGE - 2), (0, width - rows_here)))
    packet = jnp.concatenate([own_cot, ids], axis=0)
    packets = from_all(packet, "dp")
    conv, activated, mixed, seg = conv_forward(
        before, own_frames, after, segments, conv_weight, point_weight, where
    )
    mixed_all = from_all(mixed, "dp")
    cell = (places, -1, capacity, width)

    placed, table = place_packets(packets, experts, capacity)
    placed, mixed_all[0] = lax.optimization_barrier((placed, mixed_all[0]))
    tables = [table]
    cots = exchange(placed.reshape(places, -1, width), "seq").reshape(cell)
    rows = to_all_blocks(place_rows(where, tables, mixed_all, experts, capacity), "seq")
    weight_in = expert_in[0]
    weight_out = expert_out[0]
    back, gated, rows, hidden, grad_pre, grad_y, router_part = expert(
        where,
        rows,
        cots,
        (weight_in, weight_out),
        router_weight.T,
    )
    back_home = exchange(back, "seq")
    grad_wout = dot_rows(hidden, grad_y)
    grad_win = dot_rows(rows, grad_pre)
    back_home, grad_wout, grad_win = lax.optimization_barrier((back_home, grad_wout, grad_win))
    back_parts = collect(tables, back_home.reshape(-1, width), experts, capacity)
    gated_home = exchange(after_all(gated, back_parts), "seq")
    back_own = to_all(back_parts, "dp")

    core = place_here % 2
    group = place_here // 2
    groups = places // 2
    grad_mixed, grad_conv, mine, theirs = tail(
        where,
        back_own,
        own_cot,
        conv,
        activated,
        point_weight,
        before,
        own_frames,
        after,
        seg,
        router_part,
        places,
        taps,
        experts,
    )
    pieces = add_pieces(mine, swap(theirs, "seq", 1), group[None])
    pieces = [pieces[0]] + [swap(pieces[m], "seq", 2 * m) for m in range(1, groups)]
    pack_here = lax.axis_index("dp")[None]
    gated_parts = collect_packs(
        pack_here, table, gated_home.reshape(-1, width), experts, capacity
    )
    pieces, gated_parts = lax.optimization_barrier((pieces, gated_parts))
    share = sum_parts(pieces).astype(BF16)
    grad_before, grad_after = edges(grad_conv, "seq")
    frames_grad = conv_backward(grad_before, grad_conv, grad_after, seg, conv_weight, grad_mixed)
    share = sum_parts(from_all(share, "dp")).astype(BF16)
    share, frames_grad, gated_parts = lax.optimization_barrier((share, frames_grad, gated_parts))
    gated_own = exchange(gated_parts, "dp")
    gated_sum = jnp.sum(gated_own.astype(F32), axis=0)
    block_out = (mixed.astype(F32) + gated_sum).astype(BF16)
    own_half = [share] + [swap(share, "seq", 2 * m) for m in range(1, groups)]
    other_half = [swap(part, "seq", 1) for part in own_half]
    point_grad, conv_grad, router_rows = spread(
        own_half, other_half, group, core, width // places, taps, experts
    )
    router_grad = router_rows.T
    return (
        block_out[None],
        frames_grad[None],
        conv_grad,
        router_grad,
        point_grad,
        grad_win[None],
        grad_wout[None],
    )


def solution(mesh):
    placed = (
        P("dp", "seq", None),
        P("dp", None),
        P(),
        P(),
        P(),
        P("dp", "seq", None),
        P("seq", None, "dp"),
        P("seq", "dp", None),
        P("dp", "seq", None),
    )
    return jax.shard_map(
        local,
        mesh=mesh,
        in_specs=placed,
        out_specs=(
            P("dp", "seq", None),
            P("dp", "seq", None),
            P(),
            P(),
            P(),
            P("seq", None, "dp"),
            P("seq", "dp", None),
        ),
        check_vma=False,
    )
```

```python
import jax
import jax.numpy as jnp
from jax import lax
from jax.experimental import pallas as pl
from jax.experimental.pallas import tpu as pltpu
from jax.sharding import PartitionSpec as P

F32 = jnp.float32
BF16 = jnp.bfloat16
EDGE = 16
LANES = 128
SUB = 384
PARAMS = pltpu.CompilerParams(vmem_limit_bytes=56 << 20)


def shape(dims, dtype):
    return jax.ShapeDtypeStruct(dims, dtype)


def dot(a, b):
    return jnp.dot(a, b, preferred_element_type=F32)


def dot_rows(a, b):
    return lax.dot_general(a, b, (((0,), (0,)), ((), ())), preferred_element_type=F32)


def dot_last(a, b):
    return lax.dot_general(a, b, (((1,), (1,)), ((), ())), preferred_element_type=F32)


def sigmoid(value):
    return 0.5 + 0.5 * jnp.tanh(0.5 * value)


def fill_padded(scratch, before, own, after):
    rows = own.shape[0]
    scratch[0:EDGE, :] = before[...].astype(F32)
    scratch[EDGE : EDGE + rows, :] = own[...].astype(F32)
    scratch[EDGE + rows : 2 * EDGE + rows, :] = after[...].astype(F32)


def conv_forward(before, own, after, segments, weight, point, place):
    rows, width = own.shape
    length = segments.shape[1]
    taps = weight.shape[0]
    shift = EDGE - (taps - 1) // 2
    tall = rows + 2 * EDGE

    def kernel(
        place,
        before,
        own,
        after,
        segments,
        weight,
        point,
        conv_out,
        act_out,
        mixed,
        seg,
        scratch,
    ):
        fill_padded(scratch, before, own, after)
        frame = lax.broadcasted_iota(jnp.int32, (tall, length), 0) + (place[0] * rows - EDGE)
        chosen = frame == lax.broadcasted_iota(jnp.int32, (tall, length), 1)
        chosen = jnp.where(chosen, 1.0, 0.0).astype(BF16)
        numbers = jnp.broadcast_to(segments[...].astype(F32) + 1.0, (LANES, length))
        seg[...] = dot_last(chosen, numbers.astype(BF16)) - 1.0

        def column(index, carry):
            lanes = pl.ds(pl.multiple_of(index * LANES, LANES), LANES)
            seg_own = seg[EDGE : EDGE + rows, :]
            total = jnp.zeros((rows, LANES), F32)
            for tap in range(taps):
                first = tap + shift
                same = seg[first : first + rows, :] == seg_own
                piece = jnp.where(same, scratch[first : first + rows, lanes], 0.0)
                total = total + weight[tap : tap + 1, lanes] * piece
            conv_out[:, lanes] = total
            act_out[:, lanes] = (total * sigmoid(total)).astype(BF16)
            return carry

        lax.fori_loop(0, width // LANES, column, 0)
        mixed[...] = (own[...].astype(F32) + dot(act_out[...], point[...])).astype(BF16)

    return pl.pallas_call(
        kernel,
        in_specs=[pl.BlockSpec(memory_space=pltpu.SMEM)]
        + [pl.BlockSpec(memory_space=pltpu.VMEM)] * 6,
        out_shape=(
            shape((rows, width), F32),
            shape((rows, width), BF16),
            shape((rows, width), BF16),
            shape((tall, LANES), F32),
        ),
        scratch_shapes=[pltpu.VMEM((tall, width), F32)],
        compiler_params=PARAMS,
        name="conv_forward",
    )(place, before, own, after, segments, weight, point)


def conv_backward_kernel(before, own, after, seg, weight, grad_mixed, out, scratch):
    rows, width = own.shape
    taps = weight.shape[0]
    shift = EDGE - (taps - 1) // 2
    fill_padded(scratch, before, own, after)

    def column(index, carry):
        lanes = pl.ds(pl.multiple_of(index * LANES, LANES), LANES)
        seg_own = seg[EDGE : EDGE + rows, :]
        total = grad_mixed[:, lanes]
        for tap in range(taps):
            first = tap + shift
            same = seg[first : first + rows, :] == seg_own
            piece = jnp.where(same, scratch[first : first + rows, lanes], 0.0)
            total = total + weight[taps - 1 - tap : taps - tap, lanes] * piece
        out[:, lanes] = total.astype(BF16)
        return carry

    lax.fori_loop(0, width // LANES, column, 0)


def conv_backward(before, own, after, seg, weight, grad_mixed):
    rows, width = own.shape
    return pl.pallas_call(
        conv_backward_kernel,
        out_shape=shape((rows, width), BF16),
        scratch_shapes=[pltpu.VMEM((rows + 2 * EDGE, width), F32)],
        compiler_params=PARAMS,
        name="conv_backward",
    )(before, own, after, seg, weight, grad_mixed)


def tail(
    where, parts, cot, conv, act, point_w, before, own, after, seg, router_part, places, taps, experts
):
    rows, width = own.shape
    shift = EDGE - (taps - 1) // 2
    groups = places // 2
    used = width // places
    lead = -(-used // EDGE) * EDGE
    extra = -(-(taps + 1 + experts) // EDGE)
    count = len(parts)
    pieces = (groups, lead + EDGE, width)

    def kernel(where, *refs):
        parts = refs[:count]
        cot, conv, act, point_w, before, own, after, seg, router_part = refs[count : count + 9]
        grad_mixed, grad_conv, mine, theirs, scratch, shared = refs[count + 9 :]
        core = where[0] % 2
        total = cot[...].astype(F32)
        for part in parts:
            total = total + part[...].astype(F32)
        grad_mixed[...] = total
        low = total.astype(BF16)
        grad_act = dot_last(low, point_w[...])
        value = conv[...]
        sigma = sigmoid(value)
        grad_conv[...] = (grad_act * (sigma * (1.0 + value * (1.0 - sigma)))).astype(BF16)
        fill_padded(scratch, before, own, after)
        point = dot_rows(act[...], low).astype(BF16)
        for index in range(places):
            side, group = divmod(index, groups)
            shared[side, group] = jnp.zeros(pieces[1:], BF16)
            shared[side, group, 0:used, :] = point[index * used : (index + 1) * used]

        def column(index, carry):
            lanes = pl.ds(pl.multiple_of(index * LANES, LANES), LANES)
            seg_own = seg[EDGE : EDGE + rows, :]
            slope = grad_conv[:, lanes].astype(F32)
            sums = []
            for tap in range(taps):
                first = tap + shift
                same = seg[first : first + rows, :] == seg_own
                piece = jnp.where(same, scratch[first : first + rows, lanes], 0.0)
                sums.append(jnp.sum(slope * piece, axis=0, keepdims=True))
            sums.append(jnp.zeros((1, LANES), F32))
            spot = lax.broadcasted_iota(jnp.int32, (experts, LANES), 0) == where[0]
            sums.append(jnp.where(spot, router_part[0:1, lanes], 0.0))
            missing = extra * EDGE - (taps + 1 + experts)
            if missing:
                sums.append(jnp.zeros((missing, LANES), F32))
            small = jnp.concatenate(sums, axis=0).astype(BF16)
            for index in range(extra):
                side, group = divmod(index, groups)
                shared[side, group, lead : lead + EDGE, lanes] = small[
                    index * EDGE : (index + 1) * EDGE
                ]
            return carry

        lax.fori_loop(0, width // LANES, column, 0)
        mine[...] = shared[core]
        theirs[...] = shared[1 - core]

    return pl.pallas_call(
        kernel,
        in_specs=[pl.BlockSpec(memory_space=pltpu.SMEM)]
        + [pl.BlockSpec(memory_space=pltpu.VMEM)] * (count + 9),
        out_shape=(
            shape((rows, width), F32),
            shape((rows, width), BF16),
            shape(pieces, BF16),
            shape(pieces, BF16),
        ),
        scratch_shapes=[
            pltpu.VMEM((rows + 2 * EDGE, width), F32),
            pltpu.VMEM((2,) + pieces, BF16),
        ],
        compiler_params=PARAMS,
        name="tail",
    )(where, *parts, cot, conv, act, point_w, before, own, after, seg, router_part)


def table_of(ids, experts, capacity):
    rows = ids.shape[1]
    ids = ids[0:2, :].astype(F32)
    expert = lax.broadcasted_iota(jnp.int32, (experts, rows), 0).astype(F32)
    named = [jnp.where(expert == ids[j : j + 1, :], 1.0, 0.0) for j in range(2)]
    earlier = lax.broadcasted_iota(jnp.int32, (rows, rows), 0)
    earlier = earlier < lax.broadcasted_iota(jnp.int32, (rows, rows), 1)
    counts = dot((named[0] + named[1]).astype(BF16), jnp.where(earlier, 1.0, 0.0).astype(BF16))
    row = lax.broadcasted_iota(jnp.int32, (experts * capacity, rows), 0).astype(F32)
    table = jnp.zeros((experts * capacity, rows), F32)
    for j in range(2):
        slot = jnp.sum(named[j] * counts, axis=0, keepdims=True)
        table = jnp.where(row == ids[j : j + 1, :] * capacity + slot, 1.0, table)
    return table.astype(BF16)


def place_packets(packets, experts, capacity):
    count = len(packets)
    rows, width = packets[0].shape[0] - EDGE, packets[0].shape[1]
    per_expert = count * capacity

    def kernel(*refs):
        out, tables = refs[count:]
        for k, packet in enumerate(refs[:count]):
            table = table_of(packet[rows:, :rows], experts, capacity)
            tables[k] = table
            placed = dot(table, packet[:rows, :]).astype(BF16)
            for expert in range(experts):
                start = expert * per_expert + k * capacity
                piece = placed[expert * capacity : (expert + 1) * capacity]
                out[start : start + capacity, :] = piece

    return pl.pallas_call(
        kernel,
        out_shape=(
            shape((experts * per_expert, width), BF16),
            shape((count, experts * capacity, rows), BF16),
        ),
        compiler_params=PARAMS,
        name="place_packets",
    )(*packets)


def split_tables(refs, counts):
    return [ref.at[k] for ref, count in zip(refs, counts) for k in range(count)]


def place_rows(where, tables, arrays, experts, capacity, paired):
    counts = [table.shape[0] for table in tables]
    groups = len(tables)
    width = arrays[0].shape[1]
    per_expert = len(arrays) * capacity
    given = groups + len(arrays)
    held = [[k] for k in range(2 if paired else experts)]
    if paired:
        held += [[k, k + 1] for k in range(2, experts, 2)]

    def kernel(where, *refs):
        outs, scratch = refs[given:-1], refs[-1]
        here = split_tables(refs[:groups], counts)
        for k, (table, array) in enumerate(zip(here, refs[groups:given])):
            placed = dot(table[...], array[...]).astype(BF16)
            for expert in range(experts):
                piece = placed[expert * capacity : (expert + 1) * capacity]
                scratch[expert, k * capacity : (k + 1) * capacity, :] = piece
        for blocks, out in zip(held, outs):
            for low, block in enumerate(blocks):
                rows = slice(low * per_expert, (low + 1) * per_expert)
                out[rows, :] = scratch[where[0] ^ block]

    return pl.pallas_call(
        kernel,
        in_specs=[pl.BlockSpec(memory_space=pltpu.SMEM)]
        + [pl.BlockSpec(memory_space=pltpu.VMEM)] * given,
        out_shape=[shape((len(blocks) * per_expert, width), BF16) for blocks in held],
        scratch_shapes=[pltpu.VMEM((experts, per_expert, width), BF16)],
        compiler_params=PARAMS,
        name="place_rows",
    )(where, *tables, *arrays)


def collect(tables, buffer, experts, capacity):
    counts = [table.shape[0] for table in tables]
    groups = len(tables)
    rows = tables[0].shape[2]
    width = buffer.shape[1]
    per_expert = sum(counts) * capacity

    def kernel(*refs):
        buffer = refs[groups]
        here = split_tables(refs[:groups], counts)
        for k, (table, out) in enumerate(zip(here, refs[groups + 1 :])):
            starts = [expert * per_expert + k * capacity for expert in range(experts)]
            pieces = [buffer[start : start + capacity, :] for start in starts]
            out[...] = dot_rows(table[...], jnp.concatenate(pieces, axis=0)).astype(BF16)

    return pl.pallas_call(
        kernel,
        out_shape=[shape((rows, width), BF16)] * sum(counts),
        compiler_params=PARAMS,
        name="collect",
    )(*tables, buffer)


def chosen_expert(where, rows, columns, axis):
    index = lax.broadcasted_iota(jnp.int32, (rows, columns), axis)
    return jnp.where(index == where[0], 1.0, 0.0).astype(BF16)


def collect_packs(pack_here, table, buffer, experts, capacity):
    count, _, rows = table.shape
    width = buffer.shape[1]
    per_expert = count * capacity

    def kernel(pack_here, table, buffer, out):
        for k in range(count):
            starts = [expert * per_expert + k * capacity for expert in range(experts)]
            pieces = [buffer[start : start + capacity, :] for start in starts]
            summed = dot_rows(table[k], jnp.concatenate(pieces, axis=0))
            out[pack_here[0] ^ k] = summed.astype(BF16)

    return pl.pallas_call(
        kernel,
        in_specs=[pl.BlockSpec(memory_space=pltpu.SMEM)]
        + [pl.BlockSpec(memory_space=pltpu.VMEM)] * 2,
        out_shape=shape((count, rows, width), BF16),
        compiler_params=PARAMS,
        name="collect_packs",
    )(pack_here, table, buffer)


def expert(where, rows, cots, weights, router_weight):
    places, packs, capacity, width = cots.shape
    inner = weights[0].shape[1]
    experts = router_weight.shape[0]
    per_place = packs * capacity
    total = places * per_place
    group = 1
    while 2 * group * per_place <= SUB and places % (2 * group) == 0:
        group = 2 * group
    chunk = group * per_place

    def kernel(where, *refs):
        rows = refs[:places]
        cots, w_in, w_out, router = refs[places : places + 4]
        back_out, gated_out, rows_out, hidden_out, grad_pre_out, grad_y_out, router_out = refs[
            places + 4 : -1
        ]
        scratch = refs[-1]
        step = pl.program_id(0)

        @pl.when(step == 0)
        def _():
            router_out[...] = jnp.zeros_like(router_out)
            for index, ref in enumerate(rows):
                scratch[index] = ref[:per_place, :]

        inside = where[0] % group
        row = jnp.concatenate([scratch[step * group + index] for index in range(group)], axis=0)
        rows_out[...] = row
        cot = jnp.concatenate(
            [cots[inside ^ index].reshape(per_place, width) for index in range(group)], axis=0
        ).astype(F32)
        router_rows = dot(chosen_expert(where, LANES, experts, 1), router[...])
        gate = sigmoid(dot_last(row, router_rows.astype(BF16)))
        gate_wide = jnp.concatenate([gate] * (width // LANES), axis=1)
        grad_y = (gate_wide * cot).astype(BF16)
        grad_y_out[...] = grad_y
        pre = dot(row, w_in[...])
        sigma = sigmoid(pre)
        hidden = (pre * sigma).astype(BF16)
        hidden_out[...] = hidden
        slope = sigma * (1.0 + pre * (1.0 - sigma))
        grad_pre = (dot_last(grad_y, w_out[...]) * slope).astype(BF16)
        grad_pre_out[...] = grad_pre
        gated = gate_wide * dot(hidden, w_out[...])
        grad_gate = jnp.sum(cot * gated, axis=1, keepdims=True)
        grad_logit = grad_gate * (1.0 - gate)[:, 0:1]
        back = (dot_last(grad_pre, w_in[...]) + grad_logit * router_rows[0:1, :]).astype(BF16)
        gated = gated.astype(BF16)
        for index in range(group):
            piece = slice(index * per_place, (index + 1) * per_place)
            gated_out[inside ^ index] = gated[piece]
            back_out[inside ^ index] = back[piece]
        router_out[0:1, :] += jnp.sum(row.astype(F32) * grad_logit, axis=0, keepdims=True)

    def by_place(*dims):
        zeros = (0,) * len(dims)
        return pl.BlockSpec((group,) + dims, lambda i, where: (i ^ (where[0] // group),) + zeros)

    def flat(columns):
        return pl.BlockSpec((chunk, columns), lambda i, where: (i, 0))

    def full(dims):
        return pl.BlockSpec(dims, lambda i, where: (0,) * len(dims))

    return pl.pallas_call(
        kernel,
        grid_spec=pltpu.PrefetchScalarGridSpec(
            num_scalar_prefetch=1,
            grid=(places // group,),
            in_specs=[full(array.shape) for array in rows]
            + [by_place(packs, capacity, width)]
            + [full(weight.shape) for weight in weights]
            + [full(router_weight.shape)],
            out_specs=[
                by_place(per_place, width),
                by_place(per_place, width),
                flat(width),
                flat(inner),
                flat(inner),
                flat(width),
                full((8, width)),
            ],
            scratch_shapes=[pltpu.VMEM((places, per_place, width), BF16)],
        ),
        out_shape=[
            shape((places, per_place, width), BF16),
            shape((places, per_place, width), BF16),
            shape((total, width), BF16),
            shape((total, inner), BF16),
            shape((total, inner), BF16),
            shape((total, width), BF16),
            shape((8, width), F32),
        ],
        compiler_params=PARAMS,
        name="expert",
    )(where, *rows, cots, *weights, router_weight)


def add_pieces(mine, theirs, group):
    groups, size, width = mine.shape

    def kernel(group, mine, theirs, *outs):
        for index, out in enumerate(outs):
            here = group[0] ^ index
            out[...] = (mine[here].astype(F32) + theirs[here].astype(F32)).astype(BF16)

    return pl.pallas_call(
        kernel,
        in_specs=[pl.BlockSpec(memory_space=pltpu.SMEM)]
        + [pl.BlockSpec(memory_space=pltpu.VMEM)] * 2,
        out_shape=[shape((size, width), BF16)] * groups,
        compiler_params=PARAMS,
        name="add_pieces",
    )(group, mine, theirs)


def spread(own, other, group, core, used, taps, experts):
    count = len(own)
    size, width = own[0].shape

    def kernel(where, *refs):
        point, conv, router, small = refs[2 * count :]
        for index in range(2 * count):
            side = where[1] if index < count else 1 - where[1]
            place = side * count + (where[0] ^ (index % count))
            piece = refs[index][...].astype(F32)
            point[pl.ds(pl.multiple_of(place * used, 8), used), :] = piece[:used]
            small[place] = piece[size - EDGE :]
        last = -(-(taps + 1 + experts) // EDGE)
        rows = jnp.concatenate([small[place] for place in range(last)], axis=0)
        conv[...] = rows[:taps]
        router[...] = rows[taps + 1 : taps + 1 + experts]

    return pl.pallas_call(
        kernel,
        in_specs=[pl.BlockSpec(memory_space=pltpu.SMEM)]
        + [pl.BlockSpec(memory_space=pltpu.VMEM)] * (2 * count),
        out_shape=(
            shape((2 * count * used, width), F32),
            shape((taps, width), F32),
            shape((experts, width), F32),
        ),
        scratch_shapes=[pltpu.VMEM((2 * count, EDGE, width), F32)],
        compiler_params=PARAMS,
        name="spread",
    )(jnp.stack([group, core]), *own, *other)


def swap(array, axis, k):
    devices = lax.axis_size(axis)
    return lax.ppermute(array, axis, [(i, i ^ k) for i in range(devices)])


def from_all(array, axis):
    return [array] + [swap(array, axis, k) for k in range(1, lax.axis_size(axis))]


def to_all(arrays, axis):
    return [part if k == 0 else swap(part, axis, k) for k, part in enumerate(arrays)]


def exchange(array, axis):
    return lax.all_to_all(array, axis, split_axis=0, concat_axis=0, tiled=True)


def to_all_paired(arrays, axis):
    size = arrays[0].shape[0]
    rows = [arrays[0], swap(arrays[1], axis, 1)]
    for k, pair in enumerate(arrays[2:], 1):
        pair = swap(pair, axis, 2 * k)
        rows += [pair, swap(pair[size:], axis, 1)]
    return rows


def to_all_at_once(arrays, axis):
    order = jnp.arange(len(arrays), dtype=jnp.int32) ^ lax.axis_index(axis)
    moved = exchange(jnp.stack(arrays)[order], axis)[order]
    return [moved[k] for k in range(len(arrays))]


def after_all(array, others):
    return lax.optimization_barrier((array, tuple(others)))[0]


def edges(array, axis):
    devices = lax.axis_size(axis)
    up = [(i, i + 1) for i in range(devices - 1)]
    down = [(j, i) for i, j in up]
    before = lax.ppermute(array[array.shape[0] - EDGE :], axis, up)
    after = lax.ppermute(array[:EDGE], axis, down)
    return before, after


def sum_parts(parts):
    parts = [part.astype(F32) for part in parts]
    while len(parts) > 1:
        parts = [a + b for a, b in zip(parts[::2], parts[1::2])]
    return parts[0]


def local(
    frames,
    segments,
    conv_weight,
    point_weight,
    router_weight,
    expert_ids,
    expert_in,
    expert_out,
    cotangent,
):
    rows_here, width = frames.shape[1:]
    taps = conv_weight.shape[0]
    experts = router_weight.shape[1]
    capacity = -(-3 * rows_here // experts // EDGE) * EDGE
    packs = lax.axis_size("dp")
    places = lax.axis_size("seq")
    place_here = lax.axis_index("seq")
    own_frames = frames[0]
    own_cot = cotangent[0]
    before, after = edges(own_frames, "seq")

    where = place_here[None]

    ids = jnp.pad(expert_ids[0].T.astype(BF16), ((0, EDGE - 2), (0, width - rows_here)))
    packet = jnp.concatenate([own_cot, ids], axis=0)
    packets = from_all(packet, "dp")
    conv, activated, mixed, seg = conv_forward(
        before, own_frames, after, segments, conv_weight, point_weight, where
    )
    mixed_all = from_all(mixed, "dp")
    cell = (places, -1, capacity, width)

    placed, table = place_packets(packets, experts, capacity)
    placed, mixed_all[0] = lax.optimization_barrier((placed, mixed_all[0]))
    tables = [table]
    cots = exchange(placed.reshape(places, -1, width), "seq").reshape(cell)
    paired = places <= 8
    placed = place_rows(where, tables, mixed_all, experts, capacity, paired)
    rows = to_all_paired(placed, "seq") if paired else to_all_at_once(placed, "seq")
    weight_in = expert_in[0]
    weight_out = expert_out[0]
    back, gated, rows, hidden, grad_pre, grad_y, router_part = expert(
        where,
        rows,
        cots,
        (weight_in, weight_out),
        router_weight.T,
    )
    back_home = exchange(back, "seq")
    grad_wout = dot_rows(hidden, grad_y)
    grad_win = dot_rows(rows, grad_pre)
    back_home, grad_wout, grad_win = lax.optimization_barrier((back_home, grad_wout, grad_win))
    back_parts = collect(tables, back_home.reshape(-1, width), experts, capacity)
    gated_home = exchange(after_all(gated, back_parts), "seq")
    back_own = to_all(back_parts, "dp")

    core = place_here % 2
    group = place_here // 2
    groups = places // 2
    grad_mixed, grad_conv, mine, theirs = tail(
        where,
        back_own,
        own_cot,
        conv,
        activated,
        point_weight,
        before,
        own_frames,
        after,
        seg,
        router_part,
        places,
        taps,
        experts,
    )
    pieces = add_pieces(mine, swap(theirs, "seq", 1), group[None])
    pieces = [pieces[0]] + [swap(pieces[m], "seq", 2 * m) for m in range(1, groups)]
    pack_here = lax.axis_index("dp")[None]
    gated_parts = collect_packs(
        pack_here, table, gated_home.reshape(-1, width), experts, capacity
    )
    pieces, gated_parts = lax.optimization_barrier((pieces, gated_parts))
    share = sum_parts(pieces).astype(BF16)
    grad_before, grad_after = edges(grad_conv, "seq")
    frames_grad = conv_backward(grad_before, grad_conv, grad_after, seg, conv_weight, grad_mixed)
    share = sum_parts(from_all(share, "dp")).astype(BF16)
    share, frames_grad, gated_parts = lax.optimization_barrier((share, frames_grad, gated_parts))
    gated_own = exchange(gated_parts, "dp")
    gated_sum = jnp.sum(gated_own.astype(F32), axis=0)
    block_out = (mixed.astype(F32) + gated_sum).astype(BF16)
    own_half = [share] + [swap(share, "seq", 2 * m) for m in range(1, groups)]
    other_half = [swap(part, "seq", 1) for part in own_half]
    point_grad, conv_grad, router_rows = spread(
        own_half, other_half, group, core, width // places, taps, experts
    )
    router_grad = router_rows.T
    return (
        block_out[None],
        frames_grad[None],
        conv_grad,
        router_grad,
        point_grad,
        grad_win[None],
        grad_wout[None],
    )


def solution(mesh):
    placed = (
        P("dp", "seq", None),
        P("dp", None),
        P(),
        P(),
        P(),
        P("dp", "seq", None),
        P("seq", None, "dp"),
        P("seq", "dp", None),
        P("dp", "seq", None),
    )
    return jax.shard_map(
        local,
        mesh=mesh,
        in_specs=placed,
        out_specs=(
            P("dp", "seq", None),
            P("dp", "seq", None),
            P(),
            P(),
            P(),
            P("seq", None, "dp"),
            P("seq", "dp", None),
        ),
        check_vma=False,
    )
```

```python
import jax
import jax.numpy as jnp
from jax import lax
from jax.experimental import pallas as pl
from jax.experimental.pallas import tpu as pltpu
from jax.sharding import PartitionSpec as P

F32 = jnp.float32
BF16 = jnp.bfloat16
EDGE = 16
LANES = 128
SUB = 384
PARAMS = pltpu.CompilerParams(vmem_limit_bytes=56 << 20)


def shape(dims, dtype):
    return jax.ShapeDtypeStruct(dims, dtype)


def dot(a, b):
    return jnp.dot(a, b, preferred_element_type=F32)


def dot_rows(a, b):
    return lax.dot_general(a, b, (((0,), (0,)), ((), ())), preferred_element_type=F32)


def dot_last(a, b):
    return lax.dot_general(a, b, (((1,), (1,)), ((), ())), preferred_element_type=F32)


def sigmoid(value):
    return 0.5 + 0.5 * jnp.tanh(0.5 * value)


def fill_padded(scratch, before, own, after):
    rows = own.shape[0]
    scratch[0:EDGE, :] = before[...].astype(F32)
    scratch[EDGE : EDGE + rows, :] = own[...].astype(F32)
    scratch[EDGE + rows : 2 * EDGE + rows, :] = after[...].astype(F32)


def conv_forward(before, own, after, segments, weight, point, place):
    rows, width = own.shape
    length = segments.shape[1]
    taps = weight.shape[0]
    shift = EDGE - (taps - 1) // 2
    tall = rows + 2 * EDGE

    def kernel(
        place,
        before,
        own,
        after,
        segments,
        weight,
        point,
        conv_out,
        act_out,
        mixed,
        seg,
        scratch,
    ):
        fill_padded(scratch, before, own, after)
        frame = lax.broadcasted_iota(jnp.int32, (tall, length), 0) + (place[0] * rows - EDGE)
        chosen = frame == lax.broadcasted_iota(jnp.int32, (tall, length), 1)
        chosen = jnp.where(chosen, 1.0, 0.0).astype(BF16)
        numbers = jnp.broadcast_to(segments[...].astype(F32) + 1.0, (LANES, length))
        seg[...] = dot_last(chosen, numbers.astype(BF16)) - 1.0

        def column(index, carry):
            lanes = pl.ds(pl.multiple_of(index * LANES, LANES), LANES)
            seg_own = seg[EDGE : EDGE + rows, :]
            total = jnp.zeros((rows, LANES), F32)
            for tap in range(taps):
                first = tap + shift
                same = seg[first : first + rows, :] == seg_own
                piece = jnp.where(same, scratch[first : first + rows, lanes], 0.0)
                total = total + weight[tap : tap + 1, lanes] * piece
            conv_out[:, lanes] = total
            act_out[:, lanes] = (total * sigmoid(total)).astype(BF16)
            return carry

        lax.fori_loop(0, width // LANES, column, 0)
        mixed[...] = (own[...].astype(F32) + dot(act_out[...], point[...])).astype(BF16)

    return pl.pallas_call(
        kernel,
        in_specs=[pl.BlockSpec(memory_space=pltpu.SMEM)]
        + [pl.BlockSpec(memory_space=pltpu.VMEM)] * 6,
        out_shape=(
            shape((rows, width), F32),
            shape((rows, width), BF16),
            shape((rows, width), BF16),
            shape((tall, LANES), F32),
        ),
        scratch_shapes=[pltpu.VMEM((tall, width), F32)],
        compiler_params=PARAMS,
        name="conv_forward",
    )(place, before, own, after, segments, weight, point)


def conv_backward_kernel(before, own, after, seg, weight, grad_mixed, out, scratch):
    rows, width = own.shape
    taps = weight.shape[0]
    shift = EDGE - (taps - 1) // 2
    fill_padded(scratch, before, own, after)

    def column(index, carry):
        lanes = pl.ds(pl.multiple_of(index * LANES, LANES), LANES)
        seg_own = seg[EDGE : EDGE + rows, :]
        total = grad_mixed[:, lanes]
        for tap in range(taps):
            first = tap + shift
            same = seg[first : first + rows, :] == seg_own
            piece = jnp.where(same, scratch[first : first + rows, lanes], 0.0)
            total = total + weight[taps - 1 - tap : taps - tap, lanes] * piece
        out[:, lanes] = total.astype(BF16)
        return carry

    lax.fori_loop(0, width // LANES, column, 0)


def conv_backward(before, own, after, seg, weight, grad_mixed):
    rows, width = own.shape
    return pl.pallas_call(
        conv_backward_kernel,
        out_shape=shape((rows, width), BF16),
        scratch_shapes=[pltpu.VMEM((rows + 2 * EDGE, width), F32)],
        compiler_params=PARAMS,
        name="conv_backward",
    )(before, own, after, seg, weight, grad_mixed)


def tail(
    where, parts, cot, conv, act, point_w, before, own, after, seg, router_part, places, taps, experts
):
    rows, width = own.shape
    shift = EDGE - (taps - 1) // 2
    groups = places // 2
    used = width // places
    lead = -(-used // EDGE) * EDGE
    extra = -(-(taps + 1 + experts) // EDGE)
    count = len(parts)
    pieces = (groups, lead + EDGE, width)

    def kernel(where, *refs):
        parts = refs[:count]
        cot, conv, act, point_w, before, own, after, seg, router_part = refs[count : count + 9]
        grad_mixed, grad_conv, mine, theirs, scratch, shared = refs[count + 9 :]
        core = where[0] % 2
        here = where[0] // 2
        total = cot[...].astype(F32)
        for part in parts:
            total = total + part[...].astype(F32)
        grad_mixed[...] = total
        low = total.astype(BF16)
        grad_act = dot_last(low, point_w[...])
        value = conv[...]
        sigma = sigmoid(value)
        grad_conv[...] = (grad_act * (sigma * (1.0 + value * (1.0 - sigma)))).astype(BF16)
        fill_padded(scratch, before, own, after)
        point = dot_rows(act[...], low).astype(BF16)
        for index in range(places):
            side, group = divmod(index, groups)
            shared[side, group] = jnp.zeros(pieces[1:], BF16)
            shared[side, group, 0:used, :] = point[index * used : (index + 1) * used]

        def column(index, carry):
            lanes = pl.ds(pl.multiple_of(index * LANES, LANES), LANES)
            seg_own = seg[EDGE : EDGE + rows, :]
            slope = grad_conv[:, lanes].astype(F32)
            sums = []
            for tap in range(taps):
                first = tap + shift
                same = seg[first : first + rows, :] == seg_own
                piece = jnp.where(same, scratch[first : first + rows, lanes], 0.0)
                sums.append(jnp.sum(slope * piece, axis=0, keepdims=True))
            sums.append(jnp.zeros((1, LANES), F32))
            spot = lax.broadcasted_iota(jnp.int32, (experts, LANES), 0) == where[0]
            sums.append(jnp.where(spot, router_part[0:1, lanes], 0.0))
            missing = extra * EDGE - (taps + 1 + experts)
            if missing:
                sums.append(jnp.zeros((missing, LANES), F32))
            small = jnp.concatenate(sums, axis=0).astype(BF16)
            for index in range(extra):
                side, group = divmod(index, groups)
                shared[side, group, lead : lead + EDGE, lanes] = small[
                    index * EDGE : (index + 1) * EDGE
                ]
            return carry

        lax.fori_loop(0, width // LANES, column, 0)
        for index in range(groups):
            mine[index] = shared[core, here ^ index]
            theirs[index] = shared[1 - core, here ^ index]

    return pl.pallas_call(
        kernel,
        in_specs=[pl.BlockSpec(memory_space=pltpu.SMEM)]
        + [pl.BlockSpec(memory_space=pltpu.VMEM)] * (count + 9),
        out_shape=(
            shape((rows, width), F32),
            shape((rows, width), BF16),
            shape(pieces, BF16),
            shape(pieces, BF16),
        ),
        scratch_shapes=[
            pltpu.VMEM((rows + 2 * EDGE, width), F32),
            pltpu.VMEM((2,) + pieces, BF16),
        ],
        compiler_params=PARAMS,
        name="tail",
    )(where, *parts, cot, conv, act, point_w, before, own, after, seg, router_part)


def table_of(ids, experts, capacity):
    rows = ids.shape[1]
    ids = ids[0:2, :].astype(F32)
    expert = lax.broadcasted_iota(jnp.int32, (experts, rows), 0).astype(F32)
    named = [jnp.where(expert == ids[j : j + 1, :], 1.0, 0.0) for j in range(2)]
    earlier = lax.broadcasted_iota(jnp.int32, (rows, rows), 0)
    earlier = earlier < lax.broadcasted_iota(jnp.int32, (rows, rows), 1)
    counts = dot((named[0] + named[1]).astype(BF16), jnp.where(earlier, 1.0, 0.0).astype(BF16))
    row = lax.broadcasted_iota(jnp.int32, (experts * capacity, rows), 0).astype(F32)
    table = jnp.zeros((experts * capacity, rows), F32)
    for j in range(2):
        slot = jnp.sum(named[j] * counts, axis=0, keepdims=True)
        table = jnp.where(row == ids[j : j + 1, :] * capacity + slot, 1.0, table)
    return table.astype(BF16)


def place_packets(packets, experts, capacity):
    count = len(packets)
    rows, width = packets[0].shape[0] - EDGE, packets[0].shape[1]
    per_expert = count * capacity

    def kernel(*refs):
        out, tables = refs[count:]
        for k, packet in enumerate(refs[:count]):
            table = table_of(packet[rows:, :rows], experts, capacity)
            tables[k] = table
            placed = dot(table, packet[:rows, :]).astype(BF16)
            for expert in range(experts):
                start = expert * per_expert + k * capacity
                piece = placed[expert * capacity : (expert + 1) * capacity]
                out[start : start + capacity, :] = piece

    return pl.pallas_call(
        kernel,
        out_shape=(
            shape((experts * per_expert, width), BF16),
            shape((count, experts * capacity, rows), BF16),
        ),
        compiler_params=PARAMS,
        name="place_packets",
    )(*packets)


def split_tables(refs, counts):
    return [ref.at[k] for ref, count in zip(refs, counts) for k in range(count)]


def place_rows(where, tables, arrays, experts, capacity, paired):
    counts = [table.shape[0] for table in tables]
    groups = len(tables)
    width = arrays[0].shape[1]
    per_expert = len(arrays) * capacity
    given = groups + len(arrays)
    held = [[k] for k in range(2 if paired else experts)]
    if paired:
        held += [[k, k + 1] for k in range(2, experts, 2)]

    def kernel(where, *refs):
        outs, scratch = refs[given:-1], refs[-1]
        here = split_tables(refs[:groups], counts)
        for k, (table, array) in enumerate(zip(here, refs[groups:given])):
            placed = dot(table[...], array[...]).astype(BF16)
            for expert in range(experts):
                piece = placed[expert * capacity : (expert + 1) * capacity]
                scratch[expert, k * capacity : (k + 1) * capacity, :] = piece
        for blocks, out in zip(held, outs):
            for low, block in enumerate(blocks):
                rows = slice(low * per_expert, (low + 1) * per_expert)
                out[rows, :] = scratch[where[0] ^ block]

    return pl.pallas_call(
        kernel,
        in_specs=[pl.BlockSpec(memory_space=pltpu.SMEM)]
        + [pl.BlockSpec(memory_space=pltpu.VMEM)] * given,
        out_shape=[shape((len(blocks) * per_expert, width), BF16) for blocks in held],
        scratch_shapes=[pltpu.VMEM((experts, per_expert, width), BF16)],
        compiler_params=PARAMS,
        name="place_rows",
    )(where, *tables, *arrays)


def collect(tables, buffer, experts, capacity):
    counts = [table.shape[0] for table in tables]
    groups = len(tables)
    rows = tables[0].shape[2]
    width = buffer.shape[1]
    per_expert = sum(counts) * capacity

    def kernel(*refs):
        buffer = refs[groups]
        here = split_tables(refs[:groups], counts)
        for k, (table, out) in enumerate(zip(here, refs[groups + 1 :])):
            starts = [expert * per_expert + k * capacity for expert in range(experts)]
            pieces = [buffer[start : start + capacity, :] for start in starts]
            out[...] = dot_rows(table[...], jnp.concatenate(pieces, axis=0)).astype(BF16)

    return pl.pallas_call(
        kernel,
        out_shape=[shape((rows, width), BF16)] * sum(counts),
        compiler_params=PARAMS,
        name="collect",
    )(*tables, buffer)


def chosen_expert(where, rows, columns, axis):
    index = lax.broadcasted_iota(jnp.int32, (rows, columns), axis)
    return jnp.where(index == where[0], 1.0, 0.0).astype(BF16)


def collect_packs(pack_here, table, buffer, experts, capacity):
    count, _, rows = table.shape
    width = buffer.shape[1]
    per_expert = count * capacity

    def kernel(pack_here, table, buffer, out):
        for k in range(count):
            starts = [expert * per_expert + k * capacity for expert in range(experts)]
            pieces = [buffer[start : start + capacity, :] for start in starts]
            summed = dot_rows(table[k], jnp.concatenate(pieces, axis=0))
            out[pack_here[0] ^ k] = summed.astype(BF16)

    return pl.pallas_call(
        kernel,
        in_specs=[pl.BlockSpec(memory_space=pltpu.SMEM)]
        + [pl.BlockSpec(memory_space=pltpu.VMEM)] * 2,
        out_shape=shape((count, rows, width), BF16),
        compiler_params=PARAMS,
        name="collect_packs",
    )(pack_here, table, buffer)


def expert(where, rows, cots, weights, router_weight):
    places, packs, capacity, width = cots.shape
    inner = weights[0].shape[1]
    experts = router_weight.shape[0]
    per_place = packs * capacity
    total = places * per_place
    group = 1
    while 2 * group * per_place <= SUB and places % (2 * group) == 0:
        group = 2 * group
    chunk = group * per_place

    def kernel(where, *refs):
        rows = refs[:places]
        cots, w_in, w_out, router = refs[places : places + 4]
        back_out, gated_out, rows_out, hidden_out, grad_pre_out, grad_y_out, router_out = refs[
            places + 4 : -1
        ]
        scratch = refs[-1]
        step = pl.program_id(0)

        @pl.when(step == 0)
        def _():
            router_out[...] = jnp.zeros_like(router_out)
            for index, ref in enumerate(rows):
                scratch[index] = ref[:per_place, :]

        inside = where[0] % group
        row = jnp.concatenate([scratch[step * group + index] for index in range(group)], axis=0)
        rows_out[...] = row
        cot = jnp.concatenate(
            [cots[inside ^ index].reshape(per_place, width) for index in range(group)], axis=0
        ).astype(F32)
        router_rows = dot(chosen_expert(where, LANES, experts, 1), router[...])
        gate = sigmoid(dot_last(row, router_rows.astype(BF16)))
        gate_wide = jnp.concatenate([gate] * (width // LANES), axis=1)
        grad_y = (gate_wide * cot).astype(BF16)
        grad_y_out[...] = grad_y
        pre = dot(row, w_in[...])
        sigma = sigmoid(pre)
        hidden = (pre * sigma).astype(BF16)
        hidden_out[...] = hidden
        slope = sigma * (1.0 + pre * (1.0 - sigma))
        grad_pre = (dot_last(grad_y, w_out[...]) * slope).astype(BF16)
        grad_pre_out[...] = grad_pre
        gated = gate_wide * dot(hidden, w_out[...])
        grad_gate = jnp.sum(cot * gated, axis=1, keepdims=True)
        grad_logit = grad_gate * (1.0 - gate)[:, 0:1]
        back = (dot_last(grad_pre, w_in[...]) + grad_logit * router_rows[0:1, :]).astype(BF16)
        gated = gated.astype(BF16)
        for index in range(group):
            piece = slice(index * per_place, (index + 1) * per_place)
            gated_out[inside ^ index] = gated[piece]
            back_out[inside ^ index] = back[piece]
        router_out[0:1, :] += jnp.sum(row.astype(F32) * grad_logit, axis=0, keepdims=True)

    def by_place(*dims):
        zeros = (0,) * len(dims)
        return pl.BlockSpec((group,) + dims, lambda i, where: (i ^ (where[0] // group),) + zeros)

    def flat(columns):
        return pl.BlockSpec((chunk, columns), lambda i, where: (i, 0))

    def full(dims):
        return pl.BlockSpec(dims, lambda i, where: (0,) * len(dims))

    return pl.pallas_call(
        kernel,
        grid_spec=pltpu.PrefetchScalarGridSpec(
            num_scalar_prefetch=1,
            grid=(places // group,),
            in_specs=[full(array.shape) for array in rows]
            + [by_place(packs, capacity, width)]
            + [full(weight.shape) for weight in weights]
            + [full(router_weight.shape)],
            out_specs=[
                by_place(per_place, width),
                by_place(per_place, width),
                flat(width),
                flat(inner),
                flat(inner),
                flat(width),
                full((8, width)),
            ],
            scratch_shapes=[pltpu.VMEM((places, per_place, width), BF16)],
        ),
        out_shape=[
            shape((places, per_place, width), BF16),
            shape((places, per_place, width), BF16),
            shape((total, width), BF16),
            shape((total, inner), BF16),
            shape((total, inner), BF16),
            shape((total, width), BF16),
            shape((8, width), F32),
        ],
        compiler_params=PARAMS,
        name="expert",
    )(where, *rows, cots, *weights, router_weight)


def spread(own, other, group, core, used, taps, experts):
    count = len(own)
    size, width = own[0].shape

    def kernel(where, *refs):
        point, conv, router, small = refs[2 * count :]
        for index in range(2 * count):
            side = where[1] if index < count else 1 - where[1]
            place = side * count + (where[0] ^ (index % count))
            piece = refs[index][...].astype(F32)
            point[pl.ds(pl.multiple_of(place * used, 8), used), :] = piece[:used]
            small[place] = piece[size - EDGE :]
        last = -(-(taps + 1 + experts) // EDGE)
        rows = jnp.concatenate([small[place] for place in range(last)], axis=0)
        conv[...] = rows[:taps]
        router[...] = rows[taps + 1 : taps + 1 + experts]

    return pl.pallas_call(
        kernel,
        in_specs=[pl.BlockSpec(memory_space=pltpu.SMEM)]
        + [pl.BlockSpec(memory_space=pltpu.VMEM)] * (2 * count),
        out_shape=(
            shape((2 * count * used, width), F32),
            shape((taps, width), F32),
            shape((experts, width), F32),
        ),
        scratch_shapes=[pltpu.VMEM((2 * count, EDGE, width), F32)],
        compiler_params=PARAMS,
        name="spread",
    )(jnp.stack([group, core]), *own, *other)


def swap(array, axis, k):
    devices = lax.axis_size(axis)
    return lax.ppermute(array, axis, [(i, i ^ k) for i in range(devices)])


def from_all(array, axis):
    return [array] + [swap(array, axis, k) for k in range(1, lax.axis_size(axis))]


def to_all(arrays, axis):
    return [part if k == 0 else swap(part, axis, k) for k, part in enumerate(arrays)]


def exchange(array, axis):
    return lax.all_to_all(array, axis, split_axis=0, concat_axis=0, tiled=True)


def to_all_paired(arrays, axis):
    size = arrays[0].shape[0]
    rows = [arrays[0], swap(arrays[1], axis, 1)]
    for k, pair in enumerate(arrays[2:], 1):
        pair = swap(pair, axis, 2 * k)
        rows += [pair, swap(pair[size:], axis, 1)]
    return rows


def to_all_at_once(arrays, axis):
    order = jnp.arange(len(arrays), dtype=jnp.int32) ^ lax.axis_index(axis)
    moved = exchange(jnp.stack(arrays)[order], axis)[order]
    return [moved[k] for k in range(len(arrays))]


def after_all(array, others):
    return lax.optimization_barrier((array, tuple(others)))[0]


def edges(array, axis):
    devices = lax.axis_size(axis)
    up = [(i, i + 1) for i in range(devices - 1)]
    down = [(j, i) for i, j in up]
    before = lax.ppermute(array[array.shape[0] - EDGE :], axis, up)
    after = lax.ppermute(array[:EDGE], axis, down)
    return before, after


def sum_parts(parts):
    parts = [part.astype(F32) for part in parts]
    while len(parts) > 1:
        parts = [a + b for a, b in zip(parts[::2], parts[1::2])]
    return parts[0]


def local(
    frames,
    segments,
    conv_weight,
    point_weight,
    router_weight,
    expert_ids,
    expert_in,
    expert_out,
    cotangent,
):
    rows_here, width = frames.shape[1:]
    taps = conv_weight.shape[0]
    experts = router_weight.shape[1]
    capacity = -(-3 * rows_here // experts // EDGE) * EDGE
    packs = lax.axis_size("dp")
    places = lax.axis_size("seq")
    place_here = lax.axis_index("seq")
    own_frames = frames[0]
    own_cot = cotangent[0]
    before, after = edges(own_frames, "seq")

    where = place_here[None]

    ids = jnp.pad(expert_ids[0].T.astype(BF16), ((0, EDGE - 2), (0, width - rows_here)))
    packet = jnp.concatenate([own_cot, ids], axis=0)
    packets = from_all(packet, "dp")
    conv, activated, mixed, seg = conv_forward(
        before, own_frames, after, segments, conv_weight, point_weight, where
    )
    mixed_all = from_all(mixed, "dp")
    cell = (places, -1, capacity, width)

    placed, table = place_packets(packets, experts, capacity)
    placed, mixed_all[0] = lax.optimization_barrier((placed, mixed_all[0]))
    tables = [table]
    cots = exchange(placed.reshape(places, -1, width), "seq").reshape(cell)
    paired = places <= 8
    placed = place_rows(where, tables, mixed_all, experts, capacity, paired)
    rows = to_all_paired(placed, "seq") if paired else to_all_at_once(placed, "seq")
    weight_in = expert_in[0]
    weight_out = expert_out[0]
    back, gated, rows, hidden, grad_pre, grad_y, router_part = expert(
        where,
        rows,
        cots,
        (weight_in, weight_out),
        router_weight.T,
    )
    back_home = exchange(back, "seq")
    grad_wout = dot_rows(hidden, grad_y)
    grad_win = dot_rows(rows, grad_pre)
    back_home, grad_wout, grad_win = lax.optimization_barrier((back_home, grad_wout, grad_win))
    back_parts = collect(tables, back_home.reshape(-1, width), experts, capacity)
    gated_home = exchange(after_all(gated, (back_home,)), "seq")
    back_own = to_all(back_parts, "dp")

    core = place_here % 2
    group = place_here // 2
    groups = places // 2
    grad_mixed, grad_conv, mine, theirs = tail(
        where,
        back_own,
        own_cot,
        conv,
        activated,
        point_weight,
        before,
        own_frames,
        after,
        seg,
        router_part,
        places,
        taps,
        experts,
    )
    theirs = swap(theirs, "seq", 1)
    pieces = [sum_parts([mine[m], theirs[m]]).astype(BF16) for m in range(groups)]
    pieces = [pieces[0]] + [swap(pieces[m], "seq", 2 * m) for m in range(1, groups)]
    pack_here = lax.axis_index("dp")[None]
    gated_parts = collect_packs(
        pack_here, table, gated_home.reshape(-1, width), experts, capacity
    )
    pieces, gated_parts = lax.optimization_barrier((pieces, gated_parts))
    share = sum_parts(pieces).astype(BF16)
    grad_before, grad_after = edges(grad_conv, "seq")
    frames_grad = conv_backward(grad_before, grad_conv, grad_after, seg, conv_weight, grad_mixed)
    share = sum_parts(from_all(share, "dp")).astype(BF16)
    share, frames_grad, gated_parts = lax.optimization_barrier((share, frames_grad, gated_parts))
    gated_own = exchange(gated_parts, "dp")
    gated_sum = jnp.sum(gated_own.astype(F32), axis=0)
    block_out = (mixed.astype(F32) + gated_sum).astype(BF16)
    own_half = [share] + [swap(share, "seq", 2 * m) for m in range(1, groups)]
    other_half = [swap(part, "seq", 1) for part in own_half]
    point_grad, conv_grad, router_rows = spread(
        own_half, other_half, group, core, width // places, taps, experts
    )
    router_grad = router_rows.T
    return (
        block_out[None],
        frames_grad[None],
        conv_grad,
        router_grad,
        point_grad,
        grad_win[None],
        grad_wout[None],
    )


def solution(mesh):
    placed = (
        P("dp", "seq", None),
        P("dp", None),
        P(),
        P(),
        P(),
        P("dp", "seq", None),
        P("seq", None, "dp"),
        P("seq", "dp", None),
        P("dp", "seq", None),
    )
    return jax.shard_map(
        local,
        mesh=mesh,
        in_specs=placed,
        out_specs=(
            P("dp", "seq", None),
            P("dp", "seq", None),
            P(),
            P(),
            P(),
            P("seq", None, "dp"),
            P("seq", "dp", None),
        ),
        check_vma=False,
    )
```

```python
import jax
import jax.numpy as jnp
from jax import lax
from jax.experimental import pallas as pl
from jax.experimental.pallas import tpu as pltpu
from jax.sharding import PartitionSpec as P

F32 = jnp.float32
BF16 = jnp.bfloat16
EDGE = 16
LANES = 128
SUB = 384
PARAMS = pltpu.CompilerParams(vmem_limit_bytes=56 << 20)


def shape(dims, dtype):
    return jax.ShapeDtypeStruct(dims, dtype)


def dot(a, b):
    return jnp.dot(a, b, preferred_element_type=F32)


def dot_rows(a, b):
    return lax.dot_general(a, b, (((0,), (0,)), ((), ())), preferred_element_type=F32)


def dot_last(a, b):
    return lax.dot_general(a, b, (((1,), (1,)), ((), ())), preferred_element_type=F32)


def sigmoid(value):
    return 0.5 + 0.5 * jnp.tanh(0.5 * value)


def fill_padded(scratch, before, own, after):
    rows = own.shape[0]
    scratch[0:EDGE, :] = before[...].astype(F32)
    scratch[EDGE : EDGE + rows, :] = own[...].astype(F32)
    scratch[EDGE + rows : 2 * EDGE + rows, :] = after[...].astype(F32)


def conv_forward(before, own, after, segments, weight, point, place):
    rows, width = own.shape
    length = segments.shape[1]
    taps = weight.shape[0]
    shift = EDGE - (taps - 1) // 2
    tall = rows + 2 * EDGE

    def kernel(
        place,
        before,
        own,
        after,
        segments,
        weight,
        point,
        conv_out,
        act_out,
        mixed,
        seg,
        scratch,
    ):
        fill_padded(scratch, before, own, after)
        frame = lax.broadcasted_iota(jnp.int32, (tall, length), 0) + (place[0] * rows - EDGE)
        chosen = frame == lax.broadcasted_iota(jnp.int32, (tall, length), 1)
        chosen = jnp.where(chosen, 1.0, 0.0).astype(BF16)
        numbers = jnp.broadcast_to(segments[...].astype(F32) + 1.0, (LANES, length))
        seg[...] = dot_last(chosen, numbers.astype(BF16)) - 1.0

        def column(index, carry):
            lanes = pl.ds(pl.multiple_of(index * LANES, LANES), LANES)
            seg_own = seg[EDGE : EDGE + rows, :]
            total = jnp.zeros((rows, LANES), F32)
            for tap in range(taps):
                first = tap + shift
                same = seg[first : first + rows, :] == seg_own
                piece = jnp.where(same, scratch[first : first + rows, lanes], 0.0)
                total = total + weight[tap : tap + 1, lanes] * piece
            conv_out[:, lanes] = total
            act_out[:, lanes] = (total * sigmoid(total)).astype(BF16)
            return carry

        lax.fori_loop(0, width // LANES, column, 0)
        mixed[...] = (own[...].astype(F32) + dot(act_out[...], point[...])).astype(BF16)

    return pl.pallas_call(
        kernel,
        in_specs=[pl.BlockSpec(memory_space=pltpu.SMEM)]
        + [pl.BlockSpec(memory_space=pltpu.VMEM)] * 6,
        out_shape=(
            shape((rows, width), F32),
            shape((rows, width), BF16),
            shape((rows, width), BF16),
            shape((tall, LANES), F32),
        ),
        scratch_shapes=[pltpu.VMEM((tall, width), F32)],
        compiler_params=PARAMS,
        name="conv_forward",
    )(place, before, own, after, segments, weight, point)


def conv_backward_kernel(before, own, after, seg, weight, grad_mixed, out, scratch):
    rows, width = own.shape
    taps = weight.shape[0]
    shift = EDGE - (taps - 1) // 2
    fill_padded(scratch, before, own, after)

    def column(index, carry):
        lanes = pl.ds(pl.multiple_of(index * LANES, LANES), LANES)
        seg_own = seg[EDGE : EDGE + rows, :]
        total = grad_mixed[:, lanes]
        for tap in range(taps):
            first = tap + shift
            same = seg[first : first + rows, :] == seg_own
            piece = jnp.where(same, scratch[first : first + rows, lanes], 0.0)
            total = total + weight[taps - 1 - tap : taps - tap, lanes] * piece
        out[:, lanes] = total.astype(BF16)
        return carry

    lax.fori_loop(0, width // LANES, column, 0)


def conv_backward(before, own, after, seg, weight, grad_mixed):
    rows, width = own.shape
    return pl.pallas_call(
        conv_backward_kernel,
        out_shape=shape((rows, width), BF16),
        scratch_shapes=[pltpu.VMEM((rows + 2 * EDGE, width), F32)],
        compiler_params=PARAMS,
        name="conv_backward",
    )(before, own, after, seg, weight, grad_mixed)


def tail(
    where, parts, cot, conv, act, point_w, before, own, after, seg, router_part, places, taps, experts
):
    rows, width = own.shape
    shift = EDGE - (taps - 1) // 2
    groups = places // 2
    used = width // places
    lead = -(-used // EDGE) * EDGE
    extra = -(-(taps + 1 + experts) // EDGE)
    count = len(parts)
    pieces = (groups, lead + EDGE, width)

    def kernel(where, *refs):
        parts = refs[:count]
        cot, conv, act, point_w, before, own, after, seg, router_part = refs[count : count + 9]
        grad_mixed, grad_conv, mine, theirs, scratch, shared = refs[count + 9 :]
        core = where[0] % 2
        here = where[0] // 2
        total = cot[...].astype(F32)
        for part in parts:
            total = total + part[...].astype(F32)
        grad_mixed[...] = total
        low = total.astype(BF16)
        grad_act = dot_last(low, point_w[...])
        value = conv[...]
        sigma = sigmoid(value)
        grad_conv[...] = (grad_act * (sigma * (1.0 + value * (1.0 - sigma)))).astype(BF16)
        fill_padded(scratch, before, own, after)
        point = dot_rows(act[...], low).astype(BF16)
        for index in range(places):
            side, group = divmod(index, groups)
            shared[side, group] = jnp.zeros(pieces[1:], BF16)
            shared[side, group, 0:used, :] = point[index * used : (index + 1) * used]

        def column(index, carry):
            lanes = pl.ds(pl.multiple_of(index * LANES, LANES), LANES)
            seg_own = seg[EDGE : EDGE + rows, :]
            slope = grad_conv[:, lanes].astype(F32)
            sums = []
            for tap in range(taps):
                first = tap + shift
                same = seg[first : first + rows, :] == seg_own
                piece = jnp.where(same, scratch[first : first + rows, lanes], 0.0)
                sums.append(jnp.sum(slope * piece, axis=0, keepdims=True))
            sums.append(jnp.zeros((1, LANES), F32))
            spot = lax.broadcasted_iota(jnp.int32, (experts, LANES), 0) == where[0]
            sums.append(jnp.where(spot, router_part[0:1, lanes], 0.0))
            missing = extra * EDGE - (taps + 1 + experts)
            if missing:
                sums.append(jnp.zeros((missing, LANES), F32))
            small = jnp.concatenate(sums, axis=0).astype(BF16)
            for index in range(extra):
                side, group = divmod(index, groups)
                shared[side, group, lead : lead + EDGE, lanes] = small[
                    index * EDGE : (index + 1) * EDGE
                ]
            return carry

        lax.fori_loop(0, width // LANES, column, 0)
        for index in range(groups):
            mine[index] = shared[core, here ^ index]
            theirs[index] = shared[1 - core, here ^ index]

    return pl.pallas_call(
        kernel,
        in_specs=[pl.BlockSpec(memory_space=pltpu.SMEM)]
        + [pl.BlockSpec(memory_space=pltpu.VMEM)] * (count + 9),
        out_shape=(
            shape((rows, width), F32),
            shape((rows, width), BF16),
            shape(pieces, BF16),
            shape(pieces, BF16),
        ),
        scratch_shapes=[
            pltpu.VMEM((rows + 2 * EDGE, width), F32),
            pltpu.VMEM((2,) + pieces, BF16),
        ],
        compiler_params=PARAMS,
        name="tail",
    )(where, *parts, cot, conv, act, point_w, before, own, after, seg, router_part)


def table_of(ids, experts, capacity):
    rows = ids.shape[1]
    ids = ids[0:2, :].astype(F32)
    expert = lax.broadcasted_iota(jnp.int32, (experts, rows), 0).astype(F32)
    named = [jnp.where(expert == ids[j : j + 1, :], 1.0, 0.0) for j in range(2)]
    earlier = lax.broadcasted_iota(jnp.int32, (rows, rows), 0)
    earlier = earlier < lax.broadcasted_iota(jnp.int32, (rows, rows), 1)
    counts = dot((named[0] + named[1]).astype(BF16), jnp.where(earlier, 1.0, 0.0).astype(BF16))
    row = lax.broadcasted_iota(jnp.int32, (experts * capacity, rows), 0).astype(F32)
    table = jnp.zeros((experts * capacity, rows), F32)
    for j in range(2):
        slot = jnp.sum(named[j] * counts, axis=0, keepdims=True)
        table = jnp.where(row == ids[j : j + 1, :] * capacity + slot, 1.0, table)
    return table.astype(BF16)


def pack(cot, ids):
    rows, width = cot.shape

    def kernel(cot, ids, out):
        out[:rows, :] = cot[...]
        low = jnp.concatenate([ids[...].astype(F32), jnp.zeros((EDGE - 2, rows), F32)], axis=0)
        out[rows:, :] = jnp.zeros((EDGE, width), BF16)
        out[rows:, 0:rows] = low.astype(BF16)

    return pl.pallas_call(
        kernel,
        out_shape=shape((rows + EDGE, width), BF16),
        compiler_params=PARAMS,
        name="pack",
    )(cot, ids)


def place_packets(packets, experts, capacity):
    count = len(packets)
    rows, width = packets[0].shape[0] - EDGE, packets[0].shape[1]
    per_expert = count * capacity

    def kernel(*refs):
        out, tables = refs[count:]
        for k, packet in enumerate(refs[:count]):
            table = table_of(packet[rows:, :rows], experts, capacity)
            tables[k] = table
            placed = dot(table, packet[:rows, :]).astype(BF16)
            for expert in range(experts):
                start = expert * per_expert + k * capacity
                piece = placed[expert * capacity : (expert + 1) * capacity]
                out[start : start + capacity, :] = piece

    return pl.pallas_call(
        kernel,
        out_shape=(
            shape((experts * per_expert, width), BF16),
            shape((count, experts * capacity, rows), BF16),
        ),
        compiler_params=PARAMS,
        name="place_packets",
    )(*packets)


def split_tables(refs, counts):
    return [ref.at[k] for ref, count in zip(refs, counts) for k in range(count)]


def place_rows(where, tables, arrays, experts, capacity, paired):
    counts = [table.shape[0] for table in tables]
    groups = len(tables)
    width = arrays[0].shape[1]
    per_expert = len(arrays) * capacity
    given = groups + len(arrays)
    held = [[k] for k in range(2 if paired else experts)]
    if paired:
        held += [[k, k + 1] for k in range(2, experts, 2)]

    def kernel(where, *refs):
        outs, scratch = refs[given:-1], refs[-1]
        here = split_tables(refs[:groups], counts)
        for k, (table, array) in enumerate(zip(here, refs[groups:given])):
            placed = dot(table[...], array[...]).astype(BF16)
            for expert in range(experts):
                piece = placed[expert * capacity : (expert + 1) * capacity]
                scratch[expert, k * capacity : (k + 1) * capacity, :] = piece
        for blocks, out in zip(held, outs):
            for low, block in enumerate(blocks):
                rows = slice(low * per_expert, (low + 1) * per_expert)
                out[rows, :] = scratch[where[0] ^ block]

    return pl.pallas_call(
        kernel,
        in_specs=[pl.BlockSpec(memory_space=pltpu.SMEM)]
        + [pl.BlockSpec(memory_space=pltpu.VMEM)] * given,
        out_shape=[shape((len(blocks) * per_expert, width), BF16) for blocks in held],
        scratch_shapes=[pltpu.VMEM((experts, per_expert, width), BF16)],
        compiler_params=PARAMS,
        name="place_rows",
    )(where, *tables, *arrays)


def collect(tables, buffer, experts, capacity):
    counts = [table.shape[0] for table in tables]
    groups = len(tables)
    rows = tables[0].shape[2]
    width = buffer.shape[1]
    per_expert = sum(counts) * capacity

    def kernel(*refs):
        buffer = refs[groups]
        here = split_tables(refs[:groups], counts)
        for k, (table, out) in enumerate(zip(here, refs[groups + 1 :])):
            starts = [expert * per_expert + k * capacity for expert in range(experts)]
            pieces = [buffer[start : start + capacity, :] for start in starts]
            out[...] = dot_rows(table[...], jnp.concatenate(pieces, axis=0)).astype(BF16)

    return pl.pallas_call(
        kernel,
        out_shape=[shape((rows, width), BF16)] * sum(counts),
        compiler_params=PARAMS,
        name="collect",
    )(*tables, buffer)


def chosen_expert(where, rows, columns, axis):
    index = lax.broadcasted_iota(jnp.int32, (rows, columns), axis)
    return jnp.where(index == where[0], 1.0, 0.0).astype(BF16)


def collect_packs(pack_here, table, buffer, experts, capacity):
    count, _, rows = table.shape
    width = buffer.shape[1]
    per_expert = count * capacity

    def kernel(pack_here, table, buffer, out):
        for k in range(count):
            starts = [expert * per_expert + k * capacity for expert in range(experts)]
            pieces = [buffer[start : start + capacity, :] for start in starts]
            summed = dot_rows(table[k], jnp.concatenate(pieces, axis=0))
            out[pack_here[0] ^ k] = summed.astype(BF16)

    return pl.pallas_call(
        kernel,
        in_specs=[pl.BlockSpec(memory_space=pltpu.SMEM)]
        + [pl.BlockSpec(memory_space=pltpu.VMEM)] * 2,
        out_shape=shape((count, rows, width), BF16),
        compiler_params=PARAMS,
        name="collect_packs",
    )(pack_here, table, buffer)


def expert(where, rows, cots, weights, router_weight):
    places, packs, capacity, width = cots.shape
    inner = weights[0].shape[1]
    experts = router_weight.shape[0]
    per_place = packs * capacity
    total = places * per_place
    group = 1
    while 2 * group * per_place <= SUB and places % (2 * group) == 0:
        group = 2 * group
    chunk = group * per_place

    def kernel(where, *refs):
        rows = refs[:places]
        cots, w_in, w_out, router = refs[places : places + 4]
        back_out, gated_out, rows_out, hidden_out, grad_pre_out, grad_y_out, router_out = refs[
            places + 4 : -1
        ]
        scratch = refs[-1]
        step = pl.program_id(0)

        @pl.when(step == 0)
        def _():
            router_out[...] = jnp.zeros_like(router_out)
            for index, ref in enumerate(rows):
                scratch[index] = ref[:per_place, :]

        inside = where[0] % group
        row = jnp.concatenate([scratch[step * group + index] for index in range(group)], axis=0)
        rows_out[...] = row
        cot = jnp.concatenate(
            [cots[inside ^ index].reshape(per_place, width) for index in range(group)], axis=0
        ).astype(F32)
        router_rows = dot(chosen_expert(where, LANES, experts, 1), router[...])
        gate = sigmoid(dot_last(row, router_rows.astype(BF16)))
        gate_wide = jnp.concatenate([gate] * (width // LANES), axis=1)
        grad_y = (gate_wide * cot).astype(BF16)
        grad_y_out[...] = grad_y
        pre = dot(row, w_in[...])
        sigma = sigmoid(pre)
        hidden = (pre * sigma).astype(BF16)
        hidden_out[...] = hidden
        slope = sigma * (1.0 + pre * (1.0 - sigma))
        grad_pre = (dot_last(grad_y, w_out[...]) * slope).astype(BF16)
        grad_pre_out[...] = grad_pre
        gated = gate_wide * dot(hidden, w_out[...])
        grad_gate = jnp.sum(cot * gated, axis=1, keepdims=True)
        grad_logit = grad_gate * (1.0 - gate)[:, 0:1]
        back = (dot_last(grad_pre, w_in[...]) + grad_logit * router_rows[0:1, :]).astype(BF16)
        gated = gated.astype(BF16)
        for index in range(group):
            piece = slice(index * per_place, (index + 1) * per_place)
            gated_out[inside ^ index] = gated[piece]
            back_out[inside ^ index] = back[piece]
        router_out[0:1, :] += jnp.sum(row.astype(F32) * grad_logit, axis=0, keepdims=True)

    def by_place(*dims):
        zeros = (0,) * len(dims)
        return pl.BlockSpec((group,) + dims, lambda i, where: (i ^ (where[0] // group),) + zeros)

    def flat(columns):
        return pl.BlockSpec((chunk, columns), lambda i, where: (i, 0))

    def full(dims):
        return pl.BlockSpec(dims, lambda i, where: (0,) * len(dims))

    return pl.pallas_call(
        kernel,
        grid_spec=pltpu.PrefetchScalarGridSpec(
            num_scalar_prefetch=1,
            grid=(places // group,),
            in_specs=[full(array.shape) for array in rows]
            + [by_place(packs, capacity, width)]
            + [full(weight.shape) for weight in weights]
            + [full(router_weight.shape)],
            out_specs=[
                by_place(per_place, width),
                by_place(per_place, width),
                flat(width),
                flat(inner),
                flat(inner),
                flat(width),
                full((8, width)),
            ],
            scratch_shapes=[pltpu.VMEM((places, per_place, width), BF16)],
        ),
        out_shape=[
            shape((places, per_place, width), BF16),
            shape((places, per_place, width), BF16),
            shape((total, width), BF16),
            shape((total, inner), BF16),
            shape((total, inner), BF16),
            shape((total, width), BF16),
            shape((8, width), F32),
        ],
        compiler_params=PARAMS,
        name="expert",
    )(where, *rows, cots, *weights, router_weight)


def spread(own, other, group, core, used, taps, experts):
    count = len(own)
    size, width = own[0].shape

    def kernel(where, *refs):
        point, conv, router, small = refs[2 * count :]
        for index in range(2 * count):
            side = where[1] if index < count else 1 - where[1]
            place = side * count + (where[0] ^ (index % count))
            piece = refs[index][...].astype(F32)
            point[pl.ds(pl.multiple_of(place * used, 8), used), :] = piece[:used]
            small[place] = piece[size - EDGE :]
        last = -(-(taps + 1 + experts) // EDGE)
        rows = jnp.concatenate([small[place] for place in range(last)], axis=0)
        conv[...] = rows[:taps]
        router[...] = rows[taps + 1 : taps + 1 + experts]

    return pl.pallas_call(
        kernel,
        in_specs=[pl.BlockSpec(memory_space=pltpu.SMEM)]
        + [pl.BlockSpec(memory_space=pltpu.VMEM)] * (2 * count),
        out_shape=(
            shape((2 * count * used, width), F32),
            shape((taps, width), F32),
            shape((experts, width), F32),
        ),
        scratch_shapes=[pltpu.VMEM((2 * count, EDGE, width), F32)],
        compiler_params=PARAMS,
        name="spread",
    )(jnp.stack([group, core]), *own, *other)


def swap(array, axis, k):
    devices = lax.axis_size(axis)
    return lax.ppermute(array, axis, [(i, i ^ k) for i in range(devices)])


def from_all(array, axis):
    return [array] + [swap(array, axis, k) for k in range(1, lax.axis_size(axis))]


def to_all(arrays, axis):
    return [part if k == 0 else swap(part, axis, k) for k, part in enumerate(arrays)]


def exchange(array, axis):
    return lax.all_to_all(array, axis, split_axis=0, concat_axis=0, tiled=True)


def to_all_paired(arrays, axis):
    size = arrays[0].shape[0]
    rows = [arrays[0], swap(arrays[1], axis, 1)]
    for k, pair in enumerate(arrays[2:], 1):
        pair = swap(pair, axis, 2 * k)
        rows += [pair, swap(pair[size:], axis, 1)]
    return rows


def to_all_at_once(arrays, axis):
    order = jnp.arange(len(arrays), dtype=jnp.int32) ^ lax.axis_index(axis)
    moved = exchange(jnp.stack(arrays)[order], axis)[order]
    return [moved[k] for k in range(len(arrays))]


def after_all(array, others):
    return lax.optimization_barrier((array, tuple(others)))[0]


def edges(array, axis):
    devices = lax.axis_size(axis)
    up = [(i, i + 1) for i in range(devices - 1)]
    down = [(j, i) for i, j in up]
    before = lax.ppermute(array[array.shape[0] - EDGE :], axis, up)
    after = lax.ppermute(array[:EDGE], axis, down)
    return before, after


def sum_parts(parts):
    parts = [part.astype(F32) for part in parts]
    while len(parts) > 1:
        parts = [a + b for a, b in zip(parts[::2], parts[1::2])]
    return parts[0]


def local(
    frames,
    segments,
    conv_weight,
    point_weight,
    router_weight,
    expert_ids,
    expert_in,
    expert_out,
    cotangent,
):
    rows_here, width = frames.shape[1:]
    taps = conv_weight.shape[0]
    experts = router_weight.shape[1]
    capacity = -(-3 * rows_here // experts // EDGE) * EDGE
    packs = lax.axis_size("dp")
    places = lax.axis_size("seq")
    place_here = lax.axis_index("seq")
    own_frames = frames[0]
    own_cot = cotangent[0]
    before, after = edges(own_frames, "seq")

    where = place_here[None]

    packet = pack(own_cot, expert_ids[0].T)
    packets = from_all(packet, "dp")
    conv, activated, mixed, seg = conv_forward(
        before, own_frames, after, segments, conv_weight, point_weight, where
    )
    mixed_all = from_all(mixed, "dp")
    cell = (places, -1, capacity, width)

    placed, table = place_packets(packets, experts, capacity)
    placed, mixed_all[0] = lax.optimization_barrier((placed, mixed_all[0]))
    tables = [table]
    cots = exchange(placed.reshape(places, -1, width), "seq").reshape(cell)
    paired = places <= 8
    placed = place_rows(where, tables, mixed_all, experts, capacity, paired)
    rows = to_all_paired(placed, "seq") if paired else to_all_at_once(placed, "seq")
    weight_in = expert_in[0]
    weight_out = expert_out[0]
    back, gated, rows, hidden, grad_pre, grad_y, router_part = expert(
        where,
        rows,
        cots,
        (weight_in, weight_out),
        router_weight.T,
    )
    back_home = exchange(back, "seq")
    grad_wout = dot_rows(hidden, grad_y)
    grad_win = dot_rows(rows, grad_pre)
    back_home, grad_wout, grad_win = lax.optimization_barrier((back_home, grad_wout, grad_win))
    back_parts = collect(tables, back_home.reshape(-1, width), experts, capacity)
    gated_home = exchange(after_all(gated, (back_home,)), "seq")
    back_own = to_all(back_parts, "dp")

    core = place_here % 2
    group = place_here // 2
    groups = places // 2
    grad_mixed, grad_conv, mine, theirs = tail(
        where,
        back_own,
        own_cot,
        conv,
        activated,
        point_weight,
        before,
        own_frames,
        after,
        seg,
        router_part,
        places,
        taps,
        experts,
    )
    theirs = swap(theirs, "seq", 1)
    pieces = [sum_parts([mine[m], theirs[m]]).astype(BF16) for m in range(groups)]
    pieces = [pieces[0]] + [swap(pieces[m], "seq", 2 * m) for m in range(1, groups)]
    pack_here = lax.axis_index("dp")[None]
    gated_parts = collect_packs(
        pack_here, table, gated_home.reshape(-1, width), experts, capacity
    )
    pieces, gated_parts = lax.optimization_barrier((pieces, gated_parts))
    share = sum_parts(pieces).astype(BF16)
    grad_before, grad_after = edges(grad_conv, "seq")
    frames_grad = conv_backward(grad_before, grad_conv, grad_after, seg, conv_weight, grad_mixed)
    share = sum_parts(from_all(share, "dp")).astype(BF16)
    share, frames_grad, gated_parts = lax.optimization_barrier((share, frames_grad, gated_parts))
    gated_own = exchange(gated_parts, "dp")
    gated_sum = jnp.sum(gated_own.astype(F32), axis=0)
    block_out = (mixed.astype(F32) + gated_sum).astype(BF16)
    own_half = [share] + [swap(share, "seq", 2 * m) for m in range(1, groups)]
    other_half = [swap(part, "seq", 1) for part in own_half]
    point_grad, conv_grad, router_rows = spread(
        own_half, other_half, group, core, width // places, taps, experts
    )
    router_grad = router_rows.T
    return (
        block_out[None],
        frames_grad[None],
        conv_grad,
        router_grad,
        point_grad,
        grad_win[None],
        grad_wout[None],
    )


def solution(mesh):
    placed = (
        P("dp", "seq", None),
        P("dp", None),
        P(),
        P(),
        P(),
        P("dp", "seq", None),
        P("seq", None, "dp"),
        P("seq", "dp", None),
        P("dp", "seq", None),
    )
    return jax.shard_map(
        local,
        mesh=mesh,
        in_specs=placed,
        out_specs=(
            P("dp", "seq", None),
            P("dp", "seq", None),
            P(),
            P(),
            P(),
            P("seq", None, "dp"),
            P("seq", "dp", None),
        ),
        check_vma=False,
    )
```
